512 devices in a mesh: freq: 32 (over z, y_hi, core), plane: 16 (over y_lo, x).
Axes of the slice: x: 4, y: 8 (y_hi: 2, y_lo: 4; y = y_hi * 4 + y_lo), z: 8, core: 2. Of those that a mesh axis runs over, the one named last changes fastest.
Arguments:
- contrast: float32 [2, 512, 2, 512], P(None, 'plane'), may hold values from -1 to 1
- green_kernel: bfloat16 [32, 2, 2, 2, 512, 512], P('freq', None, None, None, 'plane'), may hold values from -1 to 1
- source_pos: int32 [32, 2], P('freq'), may hold values from 0 to 511
- receiver_pos: int32 [32, 2, 64], P('freq'), may hold values from 0 to 511
- measured: float32 [32, 2, 64], P('freq'), may hold values from -6 to 6
Outputs:
- new_contrast: float32 [2, 512, 2, 512], P(None, 'plane')
- new_field: float32 [32, 2, 512, 2, 512], P('freq', None, 'plane')
The draws below stay inside these ranges and needn't reach their ends.
Inputs may be any that keep to these rules, and one draw needn't show every extreme that they name: `source_pos`: row 0 is the x index and row 1 the y index of the source cell in layer 0. `receiver_pos`: row 0 holds the x indices and row 1 the y indices of the receiver cells in layer 0; receivers may coincide.
All inputs are finite; a program needn't handle non-finite values.
Results may differ from the reference program's by a relative error of at most 0.02.
Values may be sent and summed in bfloat16 or wider, within the bound.
No kernel may reach another device: no remote copies, remote signals or barrier semaphores. Data moves between devices by JAX's collectives and lax.ppermute only.
A program may use at most 64 MiB of HBM per device.

```python
import math
import jax
import jax.numpy as jnp
from jax import lax

GRID = 512
LAYERS = 2
ITERS = 2
RECV = 64
FREQS = 32


def set_ends(array, stream_key, smallest, high):
    shape = array.shape
    place = [jax.random.randint(jax.random.fold_in(stream_key, axis), (), 0, shape[axis]) for axis in range(len(shape))]
    array = array.at[tuple(place)].set(smallest)
    longest = shape.index(max(shape))
    place[longest] = (place[longest] + 1) % shape[longest]
    return array.at[tuple(place)].set(high)


def block_levels(stream_key, extent, split, low, high):
    gain = 1.0
    for axis_at, shards_of in split:
        draws = jax.random.uniform(jax.random.fold_in(jax.random.fold_in(stream_key, 6), axis_at), (shards_of,), jnp.float32, low / len(split), high / len(split))
        gain = gain * jnp.repeat(jnp.exp(draws), extent[axis_at] // shards_of).reshape((-1,) + (1,) * (len(extent) - 1 - axis_at))
    return gain


def scatter_about(stream_key, extent, spread, reach, pieces=(), held_as=jnp.bfloat16):
    factor_of = block_levels(stream_key, extent, pieces, -0.22, 0.18) if pieces else 1.0
    values = jax.random.normal(stream_key, extent, jnp.float32) * spread * factor_of
    return jnp.minimum(jnp.maximum(values, -reach), reach).astype(held_as)


def setup_inputs(seed: int = 0) -> dict:
    key_list = jax.random.split(jax.random.key(seed), 6)
    contrast = jnp.clip(jax.random.uniform(key_list[0], (2, GRID, LAYERS, GRID), jnp.float32, -1.0, 1.0) * block_levels(key_list[0], (2, GRID, LAYERS, GRID), ((1, 16),), -0.4, 0.0), -1.0, 1.0)
    green_kernel = scatter_about(key_list[1], (FREQS, 2, LAYERS, LAYERS, GRID, GRID), 0.25, 1.0, ((0, 32), (4, 16)))
    source_pos = set_ends(jax.random.randint(key_list[2], (FREQS, 2), 0, GRID), jax.random.fold_in(key_list[2], 1), 0, GRID - 1).astype(jnp.int32)
    receiver_pos = set_ends(jax.random.randint(key_list[3], (FREQS, 2, RECV), 0, GRID), jax.random.fold_in(key_list[3], 1), 0, GRID - 1).astype(jnp.int32)
    measured = scatter_about(key_list[4], (FREQS, 2, RECV), 1.0, 6.0, ((0, 32),), jnp.float32)
    return {"contrast": contrast, "green_kernel": green_kernel, "source_pos": source_pos, "receiver_pos": receiver_pos, "measured": measured}


source_gain = 3.0

def to_half(values):
    return lax.optimization_barrier(values.astype(jnp.bfloat16)).astype(jnp.float32)

def matmul_hi(left, right):
    return jnp.dot(left, right, precision=lax.Precision.HIGHEST, preferred_element_type=jnp.float32)

def make_tables(length):
    positions = jnp.arange(length, dtype=jnp.int32)
    turn_count = positions[:, None] * positions[None, :] % length
    angles = turn_count.astype(jnp.float32) * (2.0 * math.pi / length)
    norm_scale = 1.0 / math.sqrt(length)
    return (to_half(jnp.cos(angles) * norm_scale), to_half(jnp.sin(angles) * norm_scale))

def line_phase(positions, location, length):
    turn_count = positions * location % length
    angles = turn_count.astype(jnp.float32) * (2.0 * math.pi / length)
    return (jnp.cos(angles), -jnp.sin(angles))

def forward(field_real, field_imag, cos_table, sin_table):
    grid_size, layer_count, _ = field_real.shape
    in_real = to_half(field_real).reshape(grid_size * layer_count, grid_size)
    in_imag = to_half(field_imag).reshape(grid_size * layer_count, grid_size)
    mid_real = to_half(matmul_hi(in_real, cos_table) + matmul_hi(in_imag, sin_table)).reshape(grid_size, layer_count * grid_size)
    mid_imag = to_half(matmul_hi(in_imag, cos_table) - matmul_hi(in_real, sin_table)).reshape(grid_size, layer_count * grid_size)
    out_real = matmul_hi(mid_real.T, cos_table) + matmul_hi(mid_imag.T, sin_table)
    out_imag = matmul_hi(mid_imag.T, cos_table) - matmul_hi(mid_real.T, sin_table)
    return (out_real.reshape(layer_count, grid_size, grid_size), out_imag.reshape(layer_count, grid_size, grid_size))

def inverse(spec_real, spec_imag, cos_table, sin_table):
    layer_count, grid_size, _ = spec_real.shape
    in_real = to_half(spec_real).reshape(layer_count * grid_size, grid_size)
    in_imag = to_half(spec_imag).reshape(layer_count * grid_size, grid_size)
    mid_real = to_half(matmul_hi(in_real, cos_table) - matmul_hi(in_imag, sin_table))
    mid_imag = to_half(matmul_hi(in_imag, cos_table) + matmul_hi(in_real, sin_table))
    mid_real = mid_real.T.reshape(grid_size * layer_count, grid_size)
    mid_imag = mid_imag.T.reshape(grid_size * layer_count, grid_size)
    out_real = matmul_hi(mid_real, cos_table) - matmul_hi(mid_imag, sin_table)
    out_imag = matmul_hi(mid_imag, cos_table) + matmul_hi(mid_real, sin_table)
    return (out_real.reshape(grid_size, layer_count, grid_size), out_imag.reshape(grid_size, layer_count, grid_size))

def couple(kern_real, kern_imag, spec_real, spec_imag):
    high = lax.Precision.HIGHEST
    out_real = jnp.einsum('lmqk,mqk->lqk', kern_real, spec_real, precision=high) - jnp.einsum('lmqk,mqk->lqk', kern_imag, spec_imag, precision=high)
    out_imag = jnp.einsum('lmqk,mqk->lqk', kern_real, spec_imag, precision=high) + jnp.einsum('lmqk,mqk->lqk', kern_imag, spec_real, precision=high)
    return (out_real, out_imag)

def green_apply(kern_real, kern_imag, field_real, field_imag, cos_table, sin_table):
    spec_real, spec_imag = forward(field_real, field_imag, cos_table, sin_table)
    spec_real, spec_imag = couple(kern_real, kern_imag, spec_real, spec_imag)
    return inverse(spec_real, spec_imag, cos_table, sin_table)

def reference(contrast, green_kernel, source_pos, receiver_pos, measured):
    grid_size = contrast.shape[3]
    cos_table, sin_table = make_tables(grid_size)
    con_real = contrast[0]
    con_imag = contrast[1]
    positions = jnp.arange(grid_size, dtype=jnp.int32)

    def one_freq(carry, inputs):
        grad_real, grad_imag = carry
        kernel, source, receivers, observed = inputs
        kern_real = kernel[0].astype(jnp.float32)
        kern_imag = kernel[1].astype(jnp.float32)
        phase_y_real, phase_y_imag = line_phase(positions, source[1], grid_size)
        phase_x_real, phase_x_imag = line_phase(positions, source[0], grid_size)
        source_real = source_gain * (phase_y_real[:, None] * phase_x_real[None, :] - phase_y_imag[:, None] * phase_x_imag[None, :])
        source_imag = source_gain * (phase_y_real[:, None] * phase_x_imag[None, :] + phase_y_imag[:, None] * phase_x_real[None, :])
        spec_real = kern_real[:, 0] * source_real - kern_imag[:, 0] * source_imag
        spec_imag = kern_real[:, 0] * source_imag + kern_imag[:, 0] * source_real
        inc_real, inc_imag = inverse(spec_real, spec_imag, cos_table, sin_table)
        wave_real, wave_imag = (inc_real, inc_imag)
        for sweep_index in range(ITERS):
            prod_real = con_real * wave_real - con_imag * wave_imag
            prod_imag = con_real * wave_imag + con_imag * wave_real
            delta_real, delta_imag = green_apply(kern_real, kern_imag, prod_real, prod_imag, cos_table, sin_table)
            wave_real = inc_real + delta_real
            wave_imag = inc_imag + delta_imag
        misfit_real = wave_real[receivers[0], 0, receivers[1]] - observed[0]
        misfit_imag = wave_imag[receivers[0], 0, receivers[1]] - observed[1]
        recv_y_real, recv_y_imag = line_phase(positions[None, :], receivers[1][:, None], grid_size)
        recv_x_real, recv_x_imag = line_phase(positions[None, :], receivers[0][:, None], grid_size)
        mixed_real = misfit_real[:, None] * recv_y_real - misfit_imag[:, None] * recv_y_imag
        mixed_imag = misfit_real[:, None] * recv_y_imag + misfit_imag[:, None] * recv_y_real
        adj_real = matmul_hi(mixed_real.T, recv_x_real) - matmul_hi(mixed_imag.T, recv_x_imag)
        adj_imag = matmul_hi(mixed_real.T, recv_x_imag) + matmul_hi(mixed_imag.T, recv_x_real)
        back_spec_real = kern_real[0] * adj_real + kern_imag[0] * adj_imag
        back_spec_imag = kern_real[0] * adj_imag - kern_imag[0] * adj_real
        back_real, back_imag = inverse(back_spec_real, back_spec_imag, cos_table, sin_table)
        grad_real = grad_real + (wave_real * back_real + wave_imag * back_imag)
        grad_imag = grad_imag + (wave_real * back_imag - wave_imag * back_real)
        return ((grad_real, grad_imag), (inc_real, inc_imag, wave_real, wave_imag))
    zero_grad = jnp.zeros(con_real.shape, jnp.float32)
    (grad_real, grad_imag), kept = lax.scan(one_freq, (zero_grad, zero_grad), (green_kernel, source_pos, receiver_pos, measured))
    new_real = con_real - grad_real / FREQS
    new_imag = con_imag - grad_imag / FREQS

    def final(inputs):
        kernel, inc_real, inc_imag, wave_real, wave_imag = inputs
        kern_real = kernel[0].astype(jnp.float32)
        kern_imag = kernel[1].astype(jnp.float32)
        prod_real = new_real * wave_real - new_imag * wave_imag
        prod_imag = new_real * wave_imag + new_imag * wave_real
        delta_real, delta_imag = green_apply(kern_real, kern_imag, prod_real, prod_imag, cos_table, sin_table)
        return jnp.stack([inc_real + delta_real, inc_imag + delta_imag])
    new_field = lax.map(final, (green_kernel,) + tuple(kept))
    return (jnp.stack([new_real, new_imag]), new_field)
```

```python
import math

import jax
import jax.numpy as jnp
import ml_dtypes
import numpy as np
from jax import lax
from jax.experimental import pallas as pl
from jax.experimental.pallas import tpu as pltpu
from jax.sharding import Mesh
from jax.sharding import PartitionSpec as P

GRID = 512
ROWS = 32
PEERS = 16
RECV = 64
GAIN = 3.0
f32 = jnp.float32
bf16 = jnp.bfloat16


def dft_tables():
    k = np.arange(GRID, dtype=np.int64)
    angle = ((k[:, None] * k[None, :]) % GRID).astype(np.float32) * np.float32(2.0 * math.pi / GRID)
    scale = np.float32(1.0 / math.sqrt(GRID))
    both = np.stack([np.cos(angle) * scale, np.sin(angle) * scale])
    return both.astype(ml_dtypes.bfloat16)


def mm(a, b):
    return jnp.dot(a, b, preferred_element_type=f32)


def mm_nt(a, b):
    return lax.dot_general(a, b, (((1,), (1,)), ((), ())), preferred_element_type=f32)


def swap_groups(x):
    lane = lax.broadcasted_iota(jnp.int32, x[0].shape, 1)
    low = lane < 64
    even = (lane & 32) == 0
    a0 = jnp.where(low, x[0], pltpu.roll(x[2], 64, 1))
    a2 = jnp.where(low, pltpu.roll(x[0], 64, 1), x[2])
    a1 = jnp.where(low, x[1], pltpu.roll(x[3], 64, 1))
    a3 = jnp.where(low, pltpu.roll(x[1], 64, 1), x[3])
    y0 = jnp.where(even, a0, pltpu.roll(a1, 32, 1))
    y1 = jnp.where(even, pltpu.roll(a0, 96, 1), a1)
    y2 = jnp.where(even, a2, pltpu.roll(a3, 32, 1))
    y3 = jnp.where(even, pltpu.roll(a2, 96, 1), a3)
    return [y0, y1, y2, y3]


def lines_of(tiles):
    parts = [[], [], [], []]
    for g in range(4):
        swapped = swap_groups([tiles[4 * g + i, 0:ROWS, :].astype(f32) for i in range(4)])
        for j in range(4):
            parts[j].append(swapped[j])
    return jnp.concatenate([jnp.concatenate(p, axis=1) for p in parts], axis=0).astype(bf16)


def store_tiles(out, re, im):
    quarter = [re[0:ROWS], re[ROWS:], im[0:ROWS], im[ROWS:]]
    for g in range(4):
        swapped = swap_groups([q[:, 128 * g : 128 * g + 128] for q in quarter])
        for j in range(4):
            out[4 * g + j] = swapped[j].astype(bf16)


def inv_lines(lines, table):
    a = mm(lines, table[0])
    b = mm(lines, table[1])
    return a[0:64] - b[64:128], a[64:128] + b[0:64]


def fwd_lines(re, im, table):
    both = jnp.concatenate([re, im], axis=0).astype(bf16)
    a = mm(both, table[0])
    b = mm(both, table[1])
    return a[0:64] + b[64:128], a[64:128] - b[0:64]


def times(cre, cim, ure, uim):
    return cre * ure - cim * uim, cre * uim + cim * ure


def inv_spectrum(hre, him, table):
    straight = jnp.concatenate([hre, him], axis=0).astype(bf16)
    crossed = jnp.concatenate([-him, hre], axis=0).astype(bf16)
    return mm_nt(table[0], straight) + mm_nt(table[1], crossed)


def couple(kernel, fre, fim):
    hre = []
    him = []
    for lo in range(2):
        sre = None
        sim = None
        for li in range(2):
            kre = kernel[0, lo, li].astype(f32)
            kim = kernel[1, lo, li].astype(f32)
            vre = fre[ROWS * li : ROWS * li + ROWS]
            vim = fim[ROWS * li : ROWS * li + ROWS]
            pre, pim = times(kre, kim, vre, vim)
            sre = pre if sre is None else sre + pre
            sim = pim if sim is None else sim + pim
        hre.append(sre)
        him.append(sim)
    return jnp.concatenate(hre, axis=0), jnp.concatenate(him, axis=0)


def source_body(spot, kernel, table, out):
    x0 = spot[0]
    y0 = spot[1]
    first = spot[2]
    step = 2.0 * math.pi / GRID
    kx = lax.broadcasted_iota(jnp.int32, (8, GRID), 1)
    ax = ((kx * x0) & (GRID - 1)).astype(f32) * step
    ky = lax.broadcasted_iota(jnp.int32, (ROWS, 128), 0) + first
    ay = ((ky * y0) & (GRID - 1)).astype(f32) * step
    xre = jnp.cos(ax)[0:1]
    xim = -jnp.sin(ax)[0:1]
    yre = jnp.cos(ay)[:, 0:1]
    yim = -jnp.sin(ay)[:, 0:1]
    qre = GAIN * (yre * xre - yim * xim)
    qim = GAIN * (yre * xim + yim * xre)
    zre = []
    zim = []
    for lo in range(2):
        a, b = times(kernel[0, lo, 0].astype(f32), kernel[1, lo, 0].astype(f32), qre, qim)
        zre.append(a)
        zim.append(b)
    field = inv_spectrum(jnp.concatenate(zre, axis=0), jnp.concatenate(zim, axis=0), table)
    out[...] = field.astype(bf16).reshape(PEERS, ROWS, 128)


def first_line_body(tiles, contrast, table, incident, out):
    ure, uim = inv_lines(lines_of(tiles), table)
    incident[0:64] = ure
    incident[64:128] = uim
    vre, vim = times(contrast[0:64], contrast[64:128], ure, uim)
    wre, wim = fwd_lines(vre, vim, table)
    store_tiles(out, wre, wim)


def line_body(tiles, contrast, incident, table, out):
    dre, dim = inv_lines(lines_of(tiles), table)
    ure = incident[0:64] + dre
    uim = incident[64:128] + dim
    vre, vim = times(contrast[0:64], contrast[64:128], ure, uim)
    wre, wim = fwd_lines(vre, vim, table)
    store_tiles(out, wre, wim)


def spectral(tiles, kernel, table):
    turned = tiles[...].reshape(GRID, 128).astype(f32).T.astype(bf16)
    a = mm(turned, table[0])
    b = mm(turned, table[1])
    fre = a[0:64] + b[64:128]
    fim = a[64:128] - b[0:64]
    hre, him = couple(kernel, fre, fim)
    return inv_spectrum(hre, him, table).astype(bf16)


def spectral_body(tiles, kernel, table, out):
    out[...] = spectral(tiles, kernel, table).reshape(PEERS, ROWS, 128)


def picks(column):
    where = lax.broadcasted_iota(jnp.int32, (RECV, GRID), 1)
    return jnp.where(where == column, 1.0, 0.0).astype(bf16)


def own_tables(spot, table):
    first = pl.multiple_of(spot[2], ROWS)
    return table[0, pl.ds(first, ROWS), :], table[1, pl.ds(first, ROWS), :]


def sampled_body(spot, tiles, kernel, table, source, columns, out):
    field = spectral(tiles, kernel, table)
    out[:, 0:ROWS, :] = field.reshape(PEERS, ROWS, 128)
    at_x = picks(columns[:, 0:1])
    at_y = picks(columns[:, 1:2])
    taken = mm(at_x, field) + mm(at_x, source[...].reshape(GRID, 128))
    cown, sown = own_tables(spot, table)
    zero = jnp.zeros((ROWS, GRID), bf16)
    phase_re = mm_nt(at_y, jnp.concatenate([cown, zero, -sown, zero], axis=0))
    phase_im = mm_nt(at_y, jnp.concatenate([sown, zero, cown, zero], axis=0))
    terms = jnp.concatenate([taken * phase_re, taken * phase_im], axis=0)
    total = jnp.sum(terms.T, axis=0, keepdims=True)
    high = total.astype(bf16).astype(f32)
    low = total - high
    row = lax.broadcasted_iota(jnp.int32, (16, 128), 0)
    extra = jnp.where(row == 0, high, jnp.where(row == 1, low, 0.0)).astype(bf16)
    for d in range(PEERS):
        out[d, ROWS : ROWS + 16, :] = extra


def back_body(spot, tiles, kernel, table, measured, columns, out):
    sums = jnp.zeros((16, 128), f32)
    for s in range(PEERS):
        sums = sums + tiles[s, ROWS : ROWS + 16, :].astype(f32)
    misfit = sums[0:1] + sums[1:2] - measured[...]
    mre = misfit[:, 0:RECV]
    mim = misfit[:, RECV : 2 * RECV]
    at_x = picks(columns[:, 0:1])
    at_y = picks(columns[:, 1:2])
    cown, sown = own_tables(spot, table)
    yre = mm_nt(cown, at_y)
    yim = mm_nt(sown, at_y)
    mixed_re = mre * yre + mim * yim
    mixed_im = mim * yre - mre * yim
    mixed = jnp.concatenate([mixed_re, mixed_im], axis=0).astype(bf16)
    a = mm(mixed, mm(at_x, table[0]).astype(bf16))
    b = mm(mixed, mm(at_x, table[1]).astype(bf16))
    bre = (a[0:ROWS] + b[ROWS : 2 * ROWS]) * float(GRID)
    bim = (a[ROWS : 2 * ROWS] - b[0:ROWS]) * float(GRID)
    yre = []
    yim = []
    for l in range(2):
        kre = kernel[0, 0, l].astype(f32)
        kim = kernel[1, 0, l].astype(f32)
        yre.append(kre * bre + kim * bim)
        yim.append(kre * bim - kim * bre)
    field = inv_spectrum(jnp.concatenate(yre, axis=0), jnp.concatenate(yim, axis=0), table)
    out[...] = field.astype(bf16).reshape(PEERS, ROWS, 128)


def field_body(tiles, incident, table, out):
    dre, dim = inv_lines(lines_of(tiles), table)
    out[0:64] = incident[0:64] + dre
    out[64:128] = incident[64:128] + dim


def gradient_body(tiles, wave, table, out):
    bre, bim = inv_lines(lines_of(tiles), table)
    ure = wave[0:64]
    uim = wave[64:128]
    gre = (ure * bre + uim * bim).astype(bf16)
    gim = (ure * bim - uim * bre).astype(bf16)
    for s in range(PEERS):
        row = ROWS * (s // 4)
        part = gre if row < 64 else gim
        out[s] = part[row % 64 : row % 64 + ROWS, 128 * (s % 4) : 128 * (s % 4) + 128]


def share_body(arrived, out):
    total = jnp.zeros((ROWS, 128), f32)
    for s in range(PEERS):
        total = total + arrived[s].astype(f32)
    total = total.astype(bf16)
    for d in range(2 * PEERS):
        out[d] = total


def update_body(shares, contrast, wave, table, updated, out):
    freqs = 2.0 * PEERS
    for s in range(PEERS):
        z = s // 2
        core = s % 2
        row = ROWS * (s // 4)
        lane = 128 * (s % 4)
        total = shares[4 * z + core].astype(f32) + shares[4 * z + 2 + core].astype(f32)
        updated[row : row + ROWS, lane : lane + 128] = (
            contrast[row : row + ROWS, lane : lane + 128] - total / freqs
        )
    vre, vim = times(updated[0:64], updated[64:128], wave[0:64], wave[64:128])
    wre, wim = fwd_lines(vre, vim, table)
    store_tiles(out, wre, wim)


TILES = ((PEERS, ROWS, 128), bf16)
LINES = ((128, GRID), f32)
IN_VMEM = pl.BlockSpec(memory_space=pltpu.VMEM)
IN_SMEM = pl.BlockSpec(memory_space=pltpu.SMEM)


def run(body, outs, *args, scalars=0):
    many = isinstance(outs, list)
    shapes = [jax.ShapeDtypeStruct(*o) for o in (outs if many else [outs])]
    result = pl.pallas_call(
        body,
        out_shape=shapes if many else shapes[0],
        in_specs=[IN_SMEM if i < scalars else IN_VMEM for i in range(len(args))],
        out_specs=[IN_VMEM] * len(shapes) if many else IN_VMEM,
        compiler_params=pltpu.CompilerParams(vmem_limit_bytes=40 * 1024 * 1024),
    )(*args)
    return result


def exchange(blocks, axes):
    return lax.all_to_all(blocks, axes, split_axis=0, concat_axis=0, tiled=True)


def by_part_layer(field):
    return field.transpose(0, 2, 1, 3).reshape(128, GRID)


def by_row(lines):
    return lines.reshape(2, 2, ROWS, GRID).transpose(0, 2, 1, 3)


def local(contrast, green_kernel, source_pos, receiver_pos, measured):
    table = jnp.asarray(dft_tables())
    kernel = green_kernel[0]
    first = lax.axis_index("plane") * ROWS
    spot = jnp.concatenate([source_pos[0].astype(jnp.int32), first.astype(jnp.int32)[None]])
    columns = receiver_pos[0].T
    observed = measured.reshape(1, 2 * RECV)
    lines = by_part_layer(contrast)

    source = run(source_body, TILES, spot, kernel, table, scalars=1)
    arrived = exchange(source, "plane")
    incident, sent = run(first_line_body, [LINES, TILES], arrived, lines, table)
    arrived = exchange(sent, "plane")
    sent = run(spectral_body, TILES, arrived, kernel, table)
    arrived = exchange(sent, "plane")
    sent = run(line_body, TILES, arrived, lines, incident, table)
    arrived = exchange(sent, "plane")
    wide = ((PEERS, ROWS + 16, 128), bf16)
    sent = run(sampled_body, wide, spot, arrived, kernel, table, source, columns, scalars=1)
    arrived = exchange(sent, "plane")
    sent = run(back_body, TILES, spot, arrived, kernel, table, observed, columns, scalars=1)
    wave = run(field_body, LINES, arrived, incident, table)
    arrived = exchange(sent, "plane")
    sent = run(gradient_body, TILES, arrived, wave, table)
    arrived = exchange(sent, ("z", "core"))
    sent = run(share_body, ((2 * PEERS, ROWS, 128), bf16), arrived)
    arrived = exchange(sent, ("z", "yh", "core"))
    updated, sent = run(update_body, [LINES, TILES], arrived, lines, wave, table)
    arrived = exchange(sent, "plane")
    sent = run(spectral_body, TILES, arrived, kernel, table)
    arrived = exchange(sent, "plane")
    field = run(field_body, LINES, arrived, incident, table)
    return by_row(updated), by_row(field)[None]


def solution(mesh):
    freqs = mesh.shape["freq"]
    split = Mesh(
        mesh.devices.reshape(freqs // 4, 2, 2, mesh.shape["plane"]), ("z", "yh", "core", "plane")
    )
    freq = ("z", "yh", "core")
    return jax.shard_map(
        local,
        mesh=split,
        in_specs=(
            P(None, "plane", None, None),
            P(freq, None, None, None, "plane", None),
            P(freq, None),
            P(freq, None, None),
            P(freq, None, None),
        ),
        out_specs=(P(None, "plane", None, None), P(freq, None, "plane", None, None)),
        check_vma=False,
    )
```

```python
import math

import jax
import jax.numpy as jnp
import ml_dtypes
import numpy as np
from jax import lax
from jax.experimental import pallas as pl
from jax.experimental.pallas import tpu as pltpu
from jax.sharding import Mesh
from jax.sharding import PartitionSpec as P

GRID = 512
ROWS = 32
PEERS = 16
RECV = 64
GAIN = 3.0
f32 = jnp.float32
bf16 = jnp.bfloat16


def dft_tables():
    k = np.arange(GRID, dtype=np.int64)
    angle = ((k[:, None] * k[None, :]) % GRID).astype(np.float32) * np.float32(2.0 * math.pi / GRID)
    scale = np.float32(1.0 / math.sqrt(GRID))
    both = np.stack([np.cos(angle) * scale, np.sin(angle) * scale])
    return both.astype(ml_dtypes.bfloat16)


def mm(a, b):
    return jnp.dot(a, b, preferred_element_type=f32)


def mm_nt(a, b):
    return lax.dot_general(a, b, (((1,), (1,)), ((), ())), preferred_element_type=f32)


def swap_groups(x):
    lane = lax.broadcasted_iota(jnp.int32, x[0].shape, 1)
    low = lane < 64
    even = (lane & 32) == 0
    a0 = jnp.where(low, x[0], pltpu.roll(x[2], 64, 1))
    a2 = jnp.where(low, pltpu.roll(x[0], 64, 1), x[2])
    a1 = jnp.where(low, x[1], pltpu.roll(x[3], 64, 1))
    a3 = jnp.where(low, pltpu.roll(x[1], 64, 1), x[3])
    y0 = jnp.where(even, a0, pltpu.roll(a1, 32, 1))
    y1 = jnp.where(even, pltpu.roll(a0, 96, 1), a1)
    y2 = jnp.where(even, a2, pltpu.roll(a3, 32, 1))
    y3 = jnp.where(even, pltpu.roll(a2, 96, 1), a3)
    return [y0, y1, y2, y3]


def lines_of(tiles):
    parts = [[], [], [], []]
    for g in range(4):
        swapped = swap_groups([tiles[4 * g + i, 0:ROWS, :].astype(f32) for i in range(4)])
        for j in range(4):
            parts[j].append(swapped[j])
    return jnp.concatenate([jnp.concatenate(p, axis=1) for p in parts], axis=0).astype(bf16)


def store_tiles(out, re, im):
    quarter = [re[0:ROWS], re[ROWS:], im[0:ROWS], im[ROWS:]]
    for g in range(4):
        swapped = swap_groups([q[:, 128 * g : 128 * g + 128] for q in quarter])
        for j in range(4):
            out[4 * g + j] = swapped[j].astype(bf16)


def inv_lines(lines, table):
    a = mm(lines, table[0])
    b = mm(lines, table[1])
    return a[0:64] - b[64:128], a[64:128] + b[0:64]


def fwd_lines(re, im, table):
    both = jnp.concatenate([re, im], axis=0).astype(bf16)
    a = mm(both, table[0])
    b = mm(both, table[1])
    return a[0:64] + b[64:128], a[64:128] - b[0:64]


def times(cre, cim, ure, uim):
    return cre * ure - cim * uim, cre * uim + cim * ure


def inv_spectrum(hre, him, table):
    straight = jnp.concatenate([hre, him], axis=0).astype(bf16)
    crossed = jnp.concatenate([-him, hre], axis=0).astype(bf16)
    return mm_nt(table[0], straight) + mm_nt(table[1], crossed)


def couple(kernel, fre, fim):
    hre = []
    him = []
    for lo in range(2):
        sre = None
        sim = None
        for li in range(2):
            kre = kernel[0, lo, li].astype(f32)
            kim = kernel[1, lo, li].astype(f32)
            vre = fre[ROWS * li : ROWS * li + ROWS]
            vim = fim[ROWS * li : ROWS * li + ROWS]
            pre, pim = times(kre, kim, vre, vim)
            sre = pre if sre is None else sre + pre
            sim = pim if sim is None else sim + pim
        hre.append(sre)
        him.append(sim)
    return jnp.concatenate(hre, axis=0), jnp.concatenate(him, axis=0)


def source_body(spot_hbm, first, kernel_hbm, table_hbm, out, spectrum, kernel, table, spot, sems):
    copies = []
    where = pltpu.make_async_copy(spot_hbm, spot, sems.at[4])
    where.start()
    for part in range(2):
        copies.append(
            pltpu.make_async_copy(
                kernel_hbm.at[part, :, 0], kernel.at[part], sems.at[part]
            )
        )
        copies.append(
            pltpu.make_async_copy(table_hbm.at[part], table.at[part], sems.at[2 + part])
        )
    for copy in (copies[0], copies[2], copies[1], copies[3]):
        copy.start()
    where.wait()
    x0 = spot[0, 0]
    y0 = spot[0, 1]
    step = 2.0 * math.pi / GRID
    kx = lax.broadcasted_iota(jnp.int32, (8, GRID), 1)
    ax = ((kx * x0) & (GRID - 1)).astype(f32) * step
    ky = lax.broadcasted_iota(jnp.int32, (ROWS, 128), 0) + first[0]
    ay = ((ky * y0) & (GRID - 1)).astype(f32) * step
    xre = jnp.cos(ax)[0:1]
    xim = -jnp.sin(ax)[0:1]
    yre = jnp.cos(ay)[:, 0:1]
    yim = -jnp.sin(ay)[:, 0:1]
    qre = GAIN * (yre * xre - yim * xim)
    qim = GAIN * (yre * xim + yim * xre)
    copies[0].wait()
    copies[2].wait()
    zre = []
    zim = []
    for lo in range(2):
        a, b = times(kernel[0, lo].astype(f32), kernel[1, lo].astype(f32), qre, qim)
        zre.append(a)
        zim.append(b)
    zre = jnp.concatenate(zre, axis=0)
    zim = jnp.concatenate(zim, axis=0)
    straight = jnp.concatenate([zre, zim], axis=0).astype(bf16)
    crossed = jnp.concatenate([-zim, zre], axis=0).astype(bf16)
    spectrum[...] = straight
    copies[1].wait()
    field = mm_nt(table[0], straight)
    copies[3].wait()
    field = field + mm_nt(table[1], crossed)
    out[...] = field.astype(bf16).reshape(PEERS, ROWS, 128)


def by_part_layer(field, part):
    return jnp.concatenate([field[part, :, 0, :], field[part, :, 1, :]], axis=0)


def first_line_body(tiles, contrast, table, incident, lines, out):
    ure, uim = inv_lines(lines_of(tiles), table)
    incident[0:64] = ure
    incident[64:128] = uim
    cre = by_part_layer(contrast, 0)
    cim = by_part_layer(contrast, 1)
    lines[0:64] = cre
    lines[64:128] = cim
    vre, vim = times(cre, cim, ure, uim)
    wre, wim = fwd_lines(vre, vim, table)
    store_tiles(out, wre, wim)


def line_body(tiles, contrast, incident, table, out):
    dre, dim = inv_lines(lines_of(tiles), table)
    ure = incident[0:64] + dre
    uim = incident[64:128] + dim
    vre, vim = times(contrast[0:64], contrast[64:128], ure, uim)
    wre, wim = fwd_lines(vre, vim, table)
    store_tiles(out, wre, wim)


def coupled(tiles, kernel, table):
    turned = tiles[...].reshape(GRID, 128).astype(f32).T.astype(bf16)
    a = mm(turned, table[0])
    b = mm(turned, table[1])
    fre = a[0:64] + b[64:128]
    fim = a[64:128] - b[0:64]
    return couple(kernel, fre, fim)


def spectral_body(tiles, kernel, table, out):
    hre, him = coupled(tiles, kernel, table)
    field = inv_spectrum(hre, him, table)
    out[...] = field.astype(bf16).reshape(PEERS, ROWS, 128)


def sampled_body(first, tiles, kernel, table, spectrum, places, out, along_x, along_y):
    where = lax.broadcasted_iota(jnp.int32, (GRID, RECV), 0)
    at_x = jnp.where(where == places[0, 0:1, :], 1.0, 0.0).astype(bf16)
    at_y = jnp.where(where == places[0, 1:2, :], 1.0, 0.0).astype(bf16)
    start = pl.multiple_of(first[0], ROWS)
    xre = mm(table[0], at_x).astype(bf16)
    xim = mm(table[1], at_x).astype(bf16)
    yre = mm(table[0, pl.ds(start, ROWS), :], at_y)
    yim = mm(table[1, pl.ds(start, ROWS), :], at_y)
    along_x[0] = xre
    along_x[1] = xim
    along_y[0] = yre
    along_y[1] = yim
    hre, him = coupled(tiles, kernel, table)
    field = inv_spectrum(hre, him, table)
    out[:, 0:ROWS, :] = field.astype(bf16).reshape(PEERS, ROWS, 128)
    top = jnp.concatenate([hre[0:ROWS], him[0:ROWS]], axis=0).astype(bf16)
    top = jnp.concatenate([top, spectrum[0:ROWS], spectrum[64 : 64 + ROWS]], axis=0)
    a = mm(top, xre)
    b = mm(top, xim)
    a = a[0:64] + a[64:128]
    b = b[0:64] + b[64:128]
    pre = a[0:ROWS] - b[ROWS:64]
    pim = a[ROWS:64] + b[0:ROWS]
    sre = jnp.sum(pre * yre - pim * yim, axis=0, keepdims=True)
    sim = jnp.sum(pre * yim + pim * yre, axis=0, keepdims=True)
    total = jnp.concatenate([sre, sim], axis=1)
    high = total.astype(bf16).astype(f32)
    low = total - high
    row = lax.broadcasted_iota(jnp.int32, (16, 128), 0)
    extra = jnp.where(row == 0, high, jnp.where(row == 1, low, 0.0)).astype(bf16)
    for d in range(PEERS):
        out[d, ROWS : ROWS + 16, :] = extra


def back_body(tiles, kernel, table, measured, along_x, along_y, out):
    sums = jnp.zeros((16, 128), f32)
    for s in range(PEERS):
        sums = sums + tiles[s, ROWS : ROWS + 16, :].astype(f32)
    sums = sums[0:1] + sums[1:2]
    mre = sums[:, 0:RECV] - measured[0, 0:1, :]
    mim = sums[:, RECV : 2 * RECV] - measured[0, 1:2, :]
    yre = along_y[0]
    yim = along_y[1]
    mixed_re = mre * yre + mim * yim
    mixed_im = mim * yre - mre * yim
    mixed = jnp.concatenate([mixed_re, mixed_im], axis=0).astype(bf16)
    a = mm_nt(mixed, along_x[0])
    b = mm_nt(mixed, along_x[1])
    bre = (a[0:ROWS] + b[ROWS : 2 * ROWS]) * float(GRID)
    bim = (a[ROWS : 2 * ROWS] - b[0:ROWS]) * float(GRID)
    hre = []
    him = []
    for l in range(2):
        kre = kernel[0, 0, l].astype(f32)
        kim = kernel[1, 0, l].astype(f32)
        hre.append(kre * bre + kim * bim)
        him.append(kre * bim - kim * bre)
    field = inv_spectrum(jnp.concatenate(hre, axis=0), jnp.concatenate(him, axis=0), table)
    out[...] = field.astype(bf16).reshape(PEERS, ROWS, 128)


def field_body(tiles, incident, table, out):
    dre, dim = inv_lines(lines_of(tiles), table)
    for part, delta in enumerate((dre, dim)):
        total = incident[64 * part : 64 * part + 64] + delta
        for l in range(2):
            out[0, part, :, l, :] = total[ROWS * l : ROWS * l + ROWS]


def gradient_body(tiles, field_tiles, incident, table, wave, out):
    dre, dim = inv_lines(lines_of(field_tiles), table)
    ure = incident[0:64] + dre
    uim = incident[64:128] + dim
    wave[0:64] = ure
    wave[64:128] = uim
    bre, bim = inv_lines(lines_of(tiles), table)
    gre = (ure * bre + uim * bim).astype(bf16)
    gim = (ure * bim - uim * bre).astype(bf16)
    for s in range(PEERS):
        row = ROWS * (s // 4)
        part = gre if row < 64 else gim
        out[s] = part[row % 64 : row % 64 + ROWS, 128 * (s % 4) : 128 * (s % 4) + 128]


def share_body(arrived, out):
    total = jnp.zeros((ROWS, 128), f32)
    for s in range(PEERS):
        total = total + arrived[s].astype(f32)
    total = total.astype(bf16)
    for d in range(2 * PEERS):
        out[d] = total


def update_body(shares, contrast, wave, table, updated, out):
    freqs = 2.0 * PEERS
    rows = []
    for group in range(4):
        lanes = []
        for s in range(4 * group, 4 * group + 4):
            z = s // 2
            core = s % 2
            lanes.append(shares[4 * z + core].astype(f32) + shares[4 * z + 2 + core].astype(f32))
        total = jnp.concatenate(lanes, axis=1)
        new = contrast[ROWS * group : ROWS * group + ROWS] - total / freqs
        updated[group // 2, :, group % 2, :] = new
        rows.append(new)
    cre = jnp.concatenate(rows[0:2], axis=0)
    cim = jnp.concatenate(rows[2:4], axis=0)
    vre, vim = times(cre, cim, wave[0:64], wave[64:128])
    wre, wim = fwd_lines(vre, vim, table)
    store_tiles(out, wre, wim)


TILES = ((PEERS, ROWS, 128), bf16)
LINES = ((128, GRID), f32)
IN_VMEM = pl.BlockSpec(memory_space=pltpu.VMEM)
IN_SMEM = pl.BlockSpec(memory_space=pltpu.SMEM)


IN_HBM = pl.BlockSpec(memory_space=pltpu.HBM)


def run(body, outs, *args, spaces=(), scratch=()):
    many = isinstance(outs, list)
    shapes = [jax.ShapeDtypeStruct(*o) for o in (outs if many else [outs])]
    spaces = list(spaces) + [IN_VMEM] * (len(args) - len(spaces))
    return pl.pallas_call(
        body,
        out_shape=shapes if many else shapes[0],
        in_specs=spaces,
        out_specs=[IN_VMEM] * len(shapes) if many else IN_VMEM,
        scratch_shapes=scratch,
        compiler_params=pltpu.CompilerParams(vmem_limit_bytes=40 * 1024 * 1024),
    )(*args)


def exchange(blocks, axes):
    return lax.all_to_all(blocks, axes, split_axis=0, concat_axis=0, tiled=True)


def local(contrast, green_kernel, source_pos, receiver_pos, measured):
    table = jnp.asarray(dft_tables())
    kernel = green_kernel[0]
    first = (lax.axis_index("plane") * ROWS).astype(jnp.int32)[None]

    source, spectrum = run(
        source_body,
        [TILES, ((128, GRID), bf16)],
        source_pos,
        first,
        kernel,
        table,
        spaces=(IN_HBM, IN_SMEM, IN_HBM, IN_HBM),
        scratch=[
            pltpu.VMEM((2, 2, ROWS, GRID), bf16),
            pltpu.VMEM((2, GRID, GRID), bf16),
            pltpu.SMEM((1, 2), jnp.int32),
            pltpu.SemaphoreType.DMA((5,)),
        ],
    )
    arrived = exchange(source, "plane")
    incident, lines, sent = run(first_line_body, [LINES, LINES, TILES], arrived, contrast, table)
    arrived = exchange(sent, "plane")
    sent = run(spectral_body, TILES, arrived, kernel, table)
    arrived = exchange(sent, "plane")
    sent = run(line_body, TILES, arrived, lines, incident, table)
    arrived = exchange(sent, "plane")
    sent, along_x, along_y = run(
        sampled_body,
        [
            ((PEERS, ROWS + 16, 128), bf16),
            ((2, GRID, RECV), bf16),
            ((2, ROWS, RECV), f32),
        ],
        first,
        arrived,
        kernel,
        table,
        spectrum,
        receiver_pos,
        spaces=(IN_SMEM,),
    )
    field = exchange(sent, "plane")
    sent = run(back_body, TILES, field, kernel, table, measured, along_x, along_y)
    arrived = exchange(sent, "plane")
    wave, sent = run(gradient_body, [LINES, TILES], arrived, field, incident, table)
    arrived = exchange(sent, ("z", "core"))
    sent = run(share_body, ((2 * PEERS, ROWS, 128), bf16), arrived)
    arrived = exchange(sent, ("z", "yh", "core"))
    updated, sent = run(
        update_body, [(contrast.shape, f32), TILES], arrived, lines, wave, table
    )
    arrived = exchange(sent, "plane")
    sent = run(spectral_body, TILES, arrived, kernel, table)
    arrived = exchange(sent, "plane")
    field = run(field_body, ((1,) + contrast.shape, f32), arrived, incident, table)
    return updated, field


def solution(mesh):
    freqs = mesh.shape["freq"]
    split = Mesh(
        mesh.devices.reshape(freqs // 4, 2, 2, mesh.shape["plane"]), ("z", "yh", "core", "plane")
    )
    freq = ("z", "yh", "core")
    return jax.shard_map(
        local,
        mesh=split,
        in_specs=(
            P(None, "plane", None, None),
            P(freq, None, None, None, "plane", None),
            P(freq, None),
            P(freq, None, None),
            P(freq, None, None),
        ),
        out_specs=(P(None, "plane", None, None), P(freq, None, "plane", None, None)),
        check_vma=False,
    )
```

```python
import math

import jax
import jax.numpy as jnp
import ml_dtypes
import numpy as np
from jax import lax
from jax.experimental import pallas as pl
from jax.experimental.pallas import tpu as pltpu
from jax.sharding import PartitionSpec as P

GRID = 512
ROWS = 32
PEERS = 16
RECV = 64
GAIN = 3.0
f32 = jnp.float32
bf16 = jnp.bfloat16

ORDER = (4, 8, 5, 9, 7, 11, 6, 10, 0, 12, 1, 13, 3, 15, 2, 14)
AT = tuple(ORDER.index(b) for b in range(PEERS))
SHARES = tuple(2 * z + c for z in (0, 1, 7, 2, 6, 3, 5, 4) for c in (1, 0))


def dft_tables():
    k = np.arange(GRID, dtype=np.int64)
    angle = ((k[:, None] * k[None, :]) % GRID).astype(np.float32) * np.float32(2.0 * math.pi / GRID)
    scale = np.float32(1.0 / math.sqrt(GRID))
    both = np.stack([np.cos(angle) * scale, np.sin(angle) * scale])
    return both.astype(ml_dtypes.bfloat16)


def mm(a, b):
    return jnp.dot(a, b, preferred_element_type=f32)


def mm_nt(a, b):
    return lax.dot_general(a, b, (((1,), (1,)), ((), ())), preferred_element_type=f32)


def swap_groups(x):
    lane = lax.broadcasted_iota(jnp.int32, x[0].shape, 1)
    low = lane < 64
    even = (lane & 32) == 0
    a0 = jnp.where(low, x[0], pltpu.roll(x[2], 64, 1))
    a2 = jnp.where(low, pltpu.roll(x[0], 64, 1), x[2])
    a1 = jnp.where(low, x[1], pltpu.roll(x[3], 64, 1))
    a3 = jnp.where(low, pltpu.roll(x[1], 64, 1), x[3])
    y0 = jnp.where(even, a0, pltpu.roll(a1, 32, 1))
    y1 = jnp.where(even, pltpu.roll(a0, 96, 1), a1)
    y2 = jnp.where(even, a2, pltpu.roll(a3, 32, 1))
    y3 = jnp.where(even, pltpu.roll(a2, 96, 1), a3)
    return [y0, y1, y2, y3]


def lines_of(tiles):
    parts = [[], [], [], []]
    for g in range(4):
        swapped = swap_groups([tiles[AT[4 * g + i], 0:ROWS, :].astype(f32) for i in range(4)])
        for j in range(4):
            parts[j].append(swapped[j])
    return jnp.concatenate([jnp.concatenate(p, axis=1) for p in parts], axis=0).astype(bf16)


def store_tiles(out, re, im):
    quarter = [re[0:ROWS], re[ROWS:], im[0:ROWS], im[ROWS:]]
    for g in range(4):
        swapped = swap_groups([q[:, 128 * g : 128 * g + 128] for q in quarter])
        for j in range(4):
            out[AT[4 * g + j]] = swapped[j].astype(bf16)


def inv_lines(lines, table):
    a = mm(lines, table[0])
    b = mm(lines, table[1])
    return a[0:64] - b[64:128], a[64:128] + b[0:64]


def fwd_lines(re, im, table):
    both = jnp.concatenate([re, im], axis=0).astype(bf16)
    a = mm(both, table[0])
    b = mm(both, table[1])
    return a[0:64] + b[64:128], a[64:128] - b[0:64]


def times(cre, cim, ure, uim):
    return cre * ure - cim * uim, cre * uim + cim * ure


def inv_spectrum(hre, him, table):
    straight = jnp.concatenate([hre, him], axis=0).astype(bf16)
    crossed = jnp.concatenate([-him, hre], axis=0).astype(bf16)
    return mm_nt(table[0], straight) + mm_nt(table[1], crossed)


def store_blocks(out, field):
    field = field.astype(bf16)
    for d in range(PEERS):
        out[AT[d], 0:ROWS, :] = field[ROWS * d : ROWS * d + ROWS]


def couple(kernel, fre, fim):
    hre = []
    him = []
    for lo in range(2):
        sre = None
        sim = None
        for li in range(2):
            kre = kernel[0, lo, li].astype(f32)
            kim = kernel[1, lo, li].astype(f32)
            vre = fre[ROWS * li : ROWS * li + ROWS]
            vim = fim[ROWS * li : ROWS * li + ROWS]
            pre, pim = times(kre, kim, vre, vim)
            sre = pre if sre is None else sre + pre
            sim = pim if sim is None else sim + pim
        hre.append(sre)
        him.append(sim)
    return jnp.concatenate(hre, axis=0), jnp.concatenate(him, axis=0)


def source_body(
    spot_hbm,
    first,
    kernel_hbm,
    table_hbm,
    places_hbm,
    measured_hbm,
    out,
    spectrum,
    table,
    places,
    measured,
    kernel,
    spot,
    sems,
):
    copies = []
    where = pltpu.make_async_copy(spot_hbm, spot, sems.at[4])
    where.start()
    for part in range(2):
        copies.append(
            pltpu.make_async_copy(
                kernel_hbm.at[part, :, 0], kernel.at[part], sems.at[part]
            )
        )
        copies.append(
            pltpu.make_async_copy(table_hbm.at[part], table.at[part], sems.at[2 + part])
        )
    for copy in (copies[0], copies[2], copies[1], copies[3]):
        copy.start()
    extra = [
        pltpu.make_async_copy(places_hbm, places, sems.at[5]),
        pltpu.make_async_copy(measured_hbm, measured, sems.at[6]),
    ]
    for copy in extra:
        copy.start()
    where.wait()
    x0 = spot[0, 0]
    y0 = spot[0, 1]
    step = 2.0 * math.pi / GRID
    kx = lax.broadcasted_iota(jnp.int32, (8, GRID), 1)
    ax = ((kx * x0) & (GRID - 1)).astype(f32) * step
    ky = lax.broadcasted_iota(jnp.int32, (ROWS, 128), 0) + first[0]
    ay = ((ky * y0) & (GRID - 1)).astype(f32) * step
    xre = jnp.cos(ax)[0:1]
    xim = -jnp.sin(ax)[0:1]
    yre = jnp.cos(ay)[:, 0:1]
    yim = -jnp.sin(ay)[:, 0:1]
    qre = GAIN * (yre * xre - yim * xim)
    qim = GAIN * (yre * xim + yim * xre)
    copies[0].wait()
    copies[2].wait()
    zre = []
    zim = []
    for lo in range(2):
        a, b = times(kernel[0, lo].astype(f32), kernel[1, lo].astype(f32), qre, qim)
        zre.append(a)
        zim.append(b)
    zre = jnp.concatenate(zre, axis=0)
    zim = jnp.concatenate(zim, axis=0)
    straight = jnp.concatenate([zre, zim], axis=0).astype(bf16)
    crossed = jnp.concatenate([-zim, zre], axis=0).astype(bf16)
    spectrum[...] = straight
    copies[1].wait()
    field = mm_nt(table[0], straight)
    copies[3].wait()
    field = field + mm_nt(table[1], crossed)
    store_blocks(out, field)
    for copy in extra:
        copy.wait()


def by_part_layer(field, part):
    return jnp.concatenate([field[part, :, 0, :], field[part, :, 1, :]], axis=0)


def first_line_body(tiles, contrast, table, incident, lines, out):
    ure, uim = inv_lines(lines_of(tiles), table)
    incident[0:64] = ure
    incident[64:128] = uim
    cre = by_part_layer(contrast, 0)
    cim = by_part_layer(contrast, 1)
    lines[0:64] = cre
    lines[64:128] = cim
    vre, vim = times(cre, cim, ure, uim)
    wre, wim = fwd_lines(vre, vim, table)
    store_tiles(out, wre, wim)


def line_body(tiles, contrast, incident, table, out):
    dre, dim = inv_lines(lines_of(tiles), table)
    ure = incident[0:64] + dre
    uim = incident[64:128] + dim
    vre, vim = times(contrast[0:64], contrast[64:128], ure, uim)
    wre, wim = fwd_lines(vre, vim, table)
    store_tiles(out, wre, wim)


def coupled(tiles, kernel, table):
    stacked = jnp.concatenate([tiles[AT[d]] for d in range(PEERS)], axis=0)
    turned = stacked.astype(f32).T.astype(bf16)
    a = mm(turned, table[0])
    b = mm(turned, table[1])
    fre = a[0:64] + b[64:128]
    fim = a[64:128] - b[0:64]
    return couple(kernel, fre, fim)


def spectral_body(tiles, kernel, table, out):
    hre, him = coupled(tiles, kernel, table)
    field = inv_spectrum(hre, him, table)
    store_blocks(out, field)


def sampled_body(first, tiles, kernel, table, spectrum, places, out, along_x, along_y):
    where = lax.broadcasted_iota(jnp.int32, (GRID, RECV), 0)
    at_x = jnp.where(where == places[0, 0:1, :], 1.0, 0.0).astype(bf16)
    at_y = jnp.where(where == places[0, 1:2, :], 1.0, 0.0).astype(bf16)
    start = pl.multiple_of(first[0], ROWS)
    xre = mm(table[0], at_x).astype(bf16)
    xim = mm(table[1], at_x).astype(bf16)
    yre = mm(table[0, pl.ds(start, ROWS), :], at_y)
    yim = mm(table[1, pl.ds(start, ROWS), :], at_y)
    along_x[0] = xre
    along_x[1] = xim
    along_y[0] = yre
    along_y[1] = yim
    hre, him = coupled(tiles, kernel, table)
    field = inv_spectrum(hre, him, table)
    store_blocks(out, field)
    top = jnp.concatenate([hre[0:ROWS], him[0:ROWS]], axis=0).astype(bf16)
    top = jnp.concatenate([top, spectrum[0:ROWS], spectrum[64 : 64 + ROWS]], axis=0)
    a = mm(top, xre)
    b = mm(top, xim)
    a = a[0:64] + a[64:128]
    b = b[0:64] + b[64:128]
    pre = a[0:ROWS] - b[ROWS:64]
    pim = a[ROWS:64] + b[0:ROWS]
    sre = jnp.sum(pre * yre - pim * yim, axis=0, keepdims=True)
    sim = jnp.sum(pre * yim + pim * yre, axis=0, keepdims=True)
    total = jnp.concatenate([sre, sim], axis=1)
    high = total.astype(bf16).astype(f32)
    low = total - high
    row = lax.broadcasted_iota(jnp.int32, (16, 128), 0)
    extra = jnp.where(row == 0, high, jnp.where(row == 1, low, 0.0)).astype(bf16)
    for d in range(PEERS):
        out[d, ROWS : ROWS + 16, :] = extra


def back_body(tiles, kernel, table, measured, along_x, along_y, out):
    sums = jnp.zeros((16, 128), f32)
    for s in range(PEERS):
        sums = sums + tiles[s, ROWS : ROWS + 16, :].astype(f32)
    sums = sums[0:1] + sums[1:2]
    mre = sums[:, 0:RECV] - measured[0, 0:1, :]
    mim = sums[:, RECV : 2 * RECV] - measured[0, 1:2, :]
    yre = along_y[0]
    yim = along_y[1]
    mixed_re = mre * yre + mim * yim
    mixed_im = mim * yre - mre * yim
    mixed = jnp.concatenate([mixed_re, mixed_im], axis=0).astype(bf16)
    a = mm_nt(mixed, along_x[0])
    b = mm_nt(mixed, along_x[1])
    bre = (a[0:ROWS] + b[ROWS : 2 * ROWS]) * float(GRID)
    bim = (a[ROWS : 2 * ROWS] - b[0:ROWS]) * float(GRID)
    hre = []
    him = []
    for l in range(2):
        kre = kernel[0, 0, l].astype(f32)
        kim = kernel[1, 0, l].astype(f32)
        hre.append(kre * bre + kim * bim)
        him.append(kre * bim - kim * bre)
    field = inv_spectrum(jnp.concatenate(hre, axis=0), jnp.concatenate(him, axis=0), table)
    store_blocks(out, field)


def field_body(tiles, incident, table, out):
    dre, dim = inv_lines(lines_of(tiles), table)
    for part, delta in enumerate((dre, dim)):
        total = incident[64 * part : 64 * part + 64] + delta
        for l in range(2):
            out[0, part, :, l, :] = total[ROWS * l : ROWS * l + ROWS]


def gradient_body(tiles, field_tiles, incident, table, wave, out):
    dre, dim = inv_lines(lines_of(field_tiles), table)
    ure = incident[0:64] + dre
    uim = incident[64:128] + dim
    wave[0:64] = ure
    wave[64:128] = uim
    bre, bim = inv_lines(lines_of(tiles), table)
    gre = (ure * bre + uim * bim).astype(bf16)
    gim = (ure * bim - uim * bre).astype(bf16)
    for s in range(PEERS):
        row = ROWS * (s // 4)
        part = gre if row < 64 else gim
        out[SHARES.index(s)] = part[row % 64 : row % 64 + ROWS, 128 * (s % 4) : 128 * (s % 4) + 128]


def share_body(arrived, out):
    total = jnp.zeros((ROWS, 128), f32)
    for s in range(PEERS):
        total = total + arrived[s].astype(f32)
    total = total.astype(bf16)
    for d in range(2 * PEERS):
        out[d] = total


def update_body(shares, contrast, wave, table, updated, out):
    freqs = 2.0 * PEERS
    rows = []
    for group in range(4):
        lanes = []
        for s in range(4 * group, 4 * group + 4):
            z = s // 2
            core = s % 2
            lanes.append(shares[4 * z + core].astype(f32) + shares[4 * z + 2 + core].astype(f32))
        total = jnp.concatenate(lanes, axis=1)
        new = contrast[ROWS * group : ROWS * group + ROWS] - total / freqs
        updated[group // 2, :, group % 2, :] = new
        rows.append(new)
    cre = jnp.concatenate(rows[0:2], axis=0)
    cim = jnp.concatenate(rows[2:4], axis=0)
    vre, vim = times(cre, cim, wave[0:64], wave[64:128])
    wre, wim = fwd_lines(vre, vim, table)
    store_tiles(out, wre, wim)


TILES = ((PEERS, ROWS, 128), bf16)
LINES = ((128, GRID), f32)
IN_VMEM = pl.BlockSpec(memory_space=pltpu.VMEM)
IN_SMEM = pl.BlockSpec(memory_space=pltpu.SMEM)


IN_HBM = pl.BlockSpec(memory_space=pltpu.HBM)


def run(body, outs, *args, spaces=(), scratch=()):
    many = isinstance(outs, list)
    shapes = [jax.ShapeDtypeStruct(*o) for o in (outs if many else [outs])]
    spaces = list(spaces) + [IN_VMEM] * (len(args) - len(spaces))
    return pl.pallas_call(
        body,
        out_shape=shapes if many else shapes[0],
        in_specs=spaces,
        out_specs=[IN_VMEM] * len(shapes) if many else IN_VMEM,
        scratch_shapes=scratch,
        compiler_params=pltpu.CompilerParams(vmem_limit_bytes=40 * 1024 * 1024),
    )(*args)


def stay(array):
    return pltpu.with_memory_space_constraint(array, pltpu.HBM)


def exchange(blocks, axis, groups):
    return lax.all_to_all(
        blocks, axis, split_axis=0, concat_axis=0, tiled=True, axis_index_groups=groups
    )


def local(contrast, green_kernel, source_pos, receiver_pos, measured):
    table = jnp.asarray(dft_tables())
    kernel = green_kernel[0]
    first = (lax.axis_index("plane") * ROWS).astype(jnp.int32)[None]

    source, spectrum, table, places, observed = run(
        source_body,
        [
            TILES,
            ((128, GRID), bf16),
            (table.shape, bf16),
            (receiver_pos.shape, jnp.int32),
            (measured.shape, f32),
        ],
        stay(source_pos),
        first,
        stay(kernel),
        stay(table),
        stay(receiver_pos),
        stay(measured),
        spaces=(IN_HBM, IN_SMEM, IN_HBM, IN_HBM, IN_HBM, IN_HBM),
        scratch=[
            pltpu.VMEM((2, 2, ROWS, GRID), bf16),
            pltpu.SMEM((1, 2), jnp.int32),
            pltpu.SemaphoreType.DMA((7,)),
        ],
    )
    arrived = exchange(source, "plane", [list(ORDER)])
    incident, lines, sent = run(first_line_body, [LINES, LINES, TILES], arrived, contrast, table)
    arrived = exchange(sent, "plane", [list(ORDER)])
    sent = run(spectral_body, TILES, arrived, kernel, table)
    arrived = exchange(sent, "plane", [list(ORDER)])
    sent = run(line_body, TILES, arrived, lines, incident, table)
    arrived = exchange(sent, "plane", [list(ORDER)])
    sent, along_x, along_y = run(
        sampled_body,
        [
            ((PEERS, ROWS + 16, 128), bf16),
            ((2, GRID, RECV), bf16),
            ((2, ROWS, RECV), f32),
        ],
        first,
        arrived,
        kernel,
        table,
        spectrum,
        places,
        spaces=(IN_SMEM,),
    )
    field = exchange(sent, "plane", [list(ORDER)])
    sent = run(back_body, TILES, field, kernel, table, observed, along_x, along_y)
    arrived = exchange(sent, "plane", [list(ORDER)])
    wave, sent = run(gradient_body, [LINES, TILES], arrived, field, incident, table)
    arrived = exchange(sent, "freq", [[4 * (s // 2) + 2 * y + s % 2 for s in SHARES] for y in range(2)])
    sent = run(share_body, ((2 * PEERS, ROWS, 128), bf16), arrived)
    arrived = exchange(sent, "freq", None)
    updated, sent = run(
        update_body, [(contrast.shape, f32), TILES], arrived, lines, wave, table
    )
    arrived = exchange(sent, "plane", [list(ORDER)])
    sent = run(spectral_body, TILES, arrived, kernel, table)
    arrived = exchange(sent, "plane", [list(ORDER)])
    field = run(field_body, ((1,) + contrast.shape, f32), arrived, incident, table)
    return updated, field


def solution(mesh):
    return jax.shard_map(
        local,
        mesh=mesh,
        in_specs=(
            P(None, "plane", None, None),
            P("freq", None, None, None, "plane", None),
            P("freq", None),
            P("freq", None, None),
            P("freq", None, None),
        ),
        out_specs=(P(None, "plane", None, None), P("freq", None, "plane", None, None)),
        check_vma=False,
    )
```

```python
import math

import jax
import jax.numpy as jnp
import ml_dtypes
import numpy as np
from jax import lax
from jax.experimental import pallas as pl
from jax.experimental.pallas import tpu as pltpu
from jax.sharding import PartitionSpec as P

GRID = 512
ROWS = 32
PEERS = 16
RECV = 64
GAIN = 3.0
f32 = jnp.float32
bf16 = jnp.bfloat16

ORDER = (4, 8, 5, 9, 7, 11, 6, 10, 0, 12, 1, 13, 3, 15, 2, 14)
AT = tuple(ORDER.index(b) for b in range(PEERS))
SHARES = tuple(2 * z + c for z in (0, 1, 7, 2, 6, 3, 5, 4) for c in (1, 0))

FREQS = tuple(4 * z + 2 * y + c for z in (0, 4, 1, 5, 2, 6, 3, 7) for c in (1, 0) for y in (0, 1))


def dft_tables():
    k = np.arange(GRID, dtype=np.int64)
    angle = ((k[:, None] * k[None, :]) % GRID).astype(np.float32) * np.float32(2.0 * math.pi / GRID)
    scale = np.float32(1.0 / math.sqrt(GRID))
    both = np.stack([np.cos(angle) * scale, np.sin(angle) * scale])
    return both.astype(ml_dtypes.bfloat16)


def mm(a, b):
    return jnp.dot(a, b, preferred_element_type=f32)


def mm_nt(a, b):
    return lax.dot_general(a, b, (((1,), (1,)), ((), ())), preferred_element_type=f32)


def swap_groups(x):
    lane = lax.broadcasted_iota(jnp.int32, x[0].shape, 1)
    low = lane < 64
    even = (lane & 32) == 0
    a0 = jnp.where(low, x[0], pltpu.roll(x[2], 64, 1))
    a2 = jnp.where(low, pltpu.roll(x[0], 64, 1), x[2])
    a1 = jnp.where(low, x[1], pltpu.roll(x[3], 64, 1))
    a3 = jnp.where(low, pltpu.roll(x[1], 64, 1), x[3])
    y0 = jnp.where(even, a0, pltpu.roll(a1, 32, 1))
    y1 = jnp.where(even, pltpu.roll(a0, 96, 1), a1)
    y2 = jnp.where(even, a2, pltpu.roll(a3, 32, 1))
    y3 = jnp.where(even, pltpu.roll(a2, 96, 1), a3)
    return [y0, y1, y2, y3]


def lines_of(tiles):
    parts = [[], [], [], []]
    for g in range(4):
        swapped = swap_groups([tiles[AT[4 * g + i], 0:ROWS, :].astype(f32) for i in range(4)])
        for j in range(4):
            parts[j].append(swapped[j])
    return jnp.concatenate([jnp.concatenate(p, axis=1) for p in parts], axis=0).astype(bf16)


def store_tiles(out, re, im):
    quarter = [re[0:ROWS], re[ROWS:], im[0:ROWS], im[ROWS:]]
    for g in range(4):
        swapped = swap_groups([q[:, 128 * g : 128 * g + 128] for q in quarter])
        for j in range(4):
            out[AT[4 * g + j]] = swapped[j].astype(bf16)


def inv_lines(lines, table):
    a = mm(lines, table[0])
    b = mm(lines, table[1])
    return a[0:64] - b[64:128], a[64:128] + b[0:64]


def fwd_lines(re, im, table):
    both = jnp.concatenate([re, im], axis=0).astype(bf16)
    a = mm(both, table[0])
    b = mm(both, table[1])
    return a[0:64] + b[64:128], a[64:128] - b[0:64]


def times(cre, cim, ure, uim):
    return cre * ure - cim * uim, cre * uim + cim * ure


def inv_spectrum(hre, him, table):
    straight = jnp.concatenate([hre, him], axis=0).astype(bf16)
    crossed = jnp.concatenate([-him, hre], axis=0).astype(bf16)
    return mm_nt(table[0], straight) + mm_nt(table[1], crossed)


def store_blocks(out, field):
    field = field.astype(bf16)
    for d in range(PEERS):
        out[AT[d], 0:ROWS, :] = field[ROWS * d : ROWS * d + ROWS]


def couple(kernel, fre, fim):
    hre = []
    him = []
    for lo in range(2):
        sre = None
        sim = None
        for li in range(2):
            kre = kernel[0, lo, li].astype(f32)
            kim = kernel[1, lo, li].astype(f32)
            vre = fre[ROWS * li : ROWS * li + ROWS]
            vim = fim[ROWS * li : ROWS * li + ROWS]
            pre, pim = times(kre, kim, vre, vim)
            sre = pre if sre is None else sre + pre
            sim = pim if sim is None else sim + pim
        hre.append(sre)
        him.append(sim)
    return jnp.concatenate(hre, axis=0), jnp.concatenate(him, axis=0)


def source_body(
    spot_hbm,
    first,
    kernel_hbm,
    table_hbm,
    places_hbm,
    measured_hbm,
    out,
    spectrum,
    table,
    places,
    measured,
    kernel,
    spot,
    sems,
):
    copies = []
    where = pltpu.make_async_copy(spot_hbm, spot, sems.at[4])
    where.start()
    for part in range(2):
        copies.append(
            pltpu.make_async_copy(
                kernel_hbm.at[part, :, 0], kernel.at[part], sems.at[part]
            )
        )
        copies.append(
            pltpu.make_async_copy(table_hbm.at[part], table.at[part], sems.at[2 + part])
        )
    for copy in (copies[0], copies[2], copies[1], copies[3]):
        copy.start()
    extra = [
        pltpu.make_async_copy(places_hbm, places, sems.at[5]),
        pltpu.make_async_copy(measured_hbm, measured, sems.at[6]),
    ]
    for copy in extra:
        copy.start()
    where.wait()
    x0 = spot[0, 0]
    y0 = spot[0, 1]
    step = 2.0 * math.pi / GRID
    kx = lax.broadcasted_iota(jnp.int32, (8, GRID), 1)
    ax = ((kx * x0) & (GRID - 1)).astype(f32) * step
    ky = lax.broadcasted_iota(jnp.int32, (ROWS, 128), 0) + first[0]
    ay = ((ky * y0) & (GRID - 1)).astype(f32) * step
    xre = jnp.cos(ax)[0:1]
    xim = -jnp.sin(ax)[0:1]
    yre = jnp.cos(ay)[:, 0:1]
    yim = -jnp.sin(ay)[:, 0:1]
    qre = GAIN * (yre * xre - yim * xim)
    qim = GAIN * (yre * xim + yim * xre)
    copies[0].wait()
    copies[2].wait()
    zre = []
    zim = []
    for lo in range(2):
        a, b = times(kernel[0, lo].astype(f32), kernel[1, lo].astype(f32), qre, qim)
        zre.append(a)
        zim.append(b)
    zre = jnp.concatenate(zre, axis=0)
    zim = jnp.concatenate(zim, axis=0)
    straight = jnp.concatenate([zre, zim], axis=0).astype(bf16)
    crossed = jnp.concatenate([-zim, zre], axis=0).astype(bf16)
    spectrum[...] = straight
    copies[1].wait()
    field = mm_nt(table[0], straight)
    copies[3].wait()
    field = field + mm_nt(table[1], crossed)
    store_blocks(out, field)
    for copy in extra:
        copy.wait()


def by_part_layer(field, part):
    return jnp.concatenate([field[part, :, 0, :], field[part, :, 1, :]], axis=0)


def first_line_body(tiles, contrast, table, incident, lines, out):
    ure, uim = inv_lines(lines_of(tiles), table)
    incident[0:64] = ure
    incident[64:128] = uim
    cre = by_part_layer(contrast, 0)
    cim = by_part_layer(contrast, 1)
    lines[0:64] = cre
    lines[64:128] = cim
    vre, vim = times(cre, cim, ure, uim)
    wre, wim = fwd_lines(vre, vim, table)
    store_tiles(out, wre, wim)


def line_body(tiles, contrast, incident, table, out):
    dre, dim = inv_lines(lines_of(tiles), table)
    ure = incident[0:64] + dre
    uim = incident[64:128] + dim
    vre, vim = times(contrast[0:64], contrast[64:128], ure, uim)
    wre, wim = fwd_lines(vre, vim, table)
    store_tiles(out, wre, wim)


def coupled(tiles, kernel, table):
    stacked = jnp.concatenate([tiles[AT[d]] for d in range(PEERS)], axis=0)
    turned = stacked.T
    a = mm(turned, table[0])
    b = mm(turned, table[1])
    fre = a[0:64] + b[64:128]
    fim = a[64:128] - b[0:64]
    return couple(kernel, fre, fim)


def spectral_body(tiles, kernel, table, out):
    hre, him = coupled(tiles, kernel, table)
    field = inv_spectrum(hre, him, table)
    store_blocks(out, field)


def sampled_body(first, tiles, kernel, table, spectrum, places, out, along_x, along_y):
    where = lax.broadcasted_iota(jnp.int32, (GRID, RECV), 0)
    at_x = jnp.where(where == places[0, 0:1, :], 1.0, 0.0).astype(bf16)
    at_y = jnp.where(where == places[0, 1:2, :], 1.0, 0.0).astype(bf16)
    start = pl.multiple_of(first[0], ROWS)
    xre = mm(table[0], at_x).astype(bf16)
    xim = mm(table[1], at_x).astype(bf16)
    yre = mm(table[0, pl.ds(start, ROWS), :], at_y)
    yim = mm(table[1, pl.ds(start, ROWS), :], at_y)
    along_x[0] = xre
    along_x[1] = xim
    along_y[0] = yre
    along_y[1] = yim
    hre, him = coupled(tiles, kernel, table)
    field = inv_spectrum(hre, him, table)
    store_blocks(out, field)
    top = jnp.concatenate([hre[0:ROWS], him[0:ROWS]], axis=0).astype(bf16)
    top = jnp.concatenate([top, spectrum[0:ROWS], spectrum[64 : 64 + ROWS]], axis=0)
    a = mm(top, xre)
    b = mm(top, xim)
    a = a[0:64] + a[64:128]
    b = b[0:64] + b[64:128]
    pre = a[0:ROWS] - b[ROWS:64]
    pim = a[ROWS:64] + b[0:ROWS]
    sre = jnp.sum(pre * yre - pim * yim, axis=0, keepdims=True)
    sim = jnp.sum(pre * yim + pim * yre, axis=0, keepdims=True)
    total = jnp.concatenate([sre, sim], axis=1)
    high = total.astype(bf16).astype(f32)
    low = total - high
    row = lax.broadcasted_iota(jnp.int32, (8, 128), 0)
    extra = jnp.where(row == 0, high, jnp.where(row == 1, low, 0.0)).astype(bf16)
    for d in range(PEERS):
        out[d, ROWS : ROWS + 8, :] = extra


def back_body(tiles, kernel, table, measured, along_x, along_y, out):
    sums = jnp.zeros((8, 128), f32)
    for s in range(PEERS):
        sums = sums + tiles[s, ROWS : ROWS + 8, :].astype(f32)
    sums = sums[0:1] + sums[1:2]
    mre = sums[:, 0:RECV] - measured[0, 0:1, :]
    mim = sums[:, RECV : 2 * RECV] - measured[0, 1:2, :]
    yre = along_y[0]
    yim = along_y[1]
    mixed_re = mre * yre + mim * yim
    mixed_im = mim * yre - mre * yim
    mixed = jnp.concatenate([mixed_re, mixed_im], axis=0).astype(bf16)
    a = mm_nt(mixed, along_x[0])
    b = mm_nt(mixed, along_x[1])
    bre = (a[0:ROWS] + b[ROWS : 2 * ROWS]) * float(GRID)
    bim = (a[ROWS : 2 * ROWS] - b[0:ROWS]) * float(GRID)
    hre = []
    him = []
    for l in range(2):
        kre = kernel[0, 0, l].astype(f32)
        kim = kernel[1, 0, l].astype(f32)
        hre.append(kre * bre + kim * bim)
        him.append(kre * bim - kim * bre)
    field = inv_spectrum(jnp.concatenate(hre, axis=0), jnp.concatenate(him, axis=0), table)
    store_blocks(out, field)


def field_body(tiles, incident, table, out):
    dre, dim = inv_lines(lines_of(tiles), table)
    for part, delta in enumerate((dre, dim)):
        total = incident[64 * part : 64 * part + 64] + delta
        for l in range(2):
            out[0, part, :, l, :] = total[ROWS * l : ROWS * l + ROWS]


def gradient_body(tiles, field_tiles, incident, table, wave, out):
    dre, dim = inv_lines(lines_of(field_tiles), table)
    ure = incident[0:64] + dre
    uim = incident[64:128] + dim
    wave[0:64] = ure
    wave[64:128] = uim
    bre, bim = inv_lines(lines_of(tiles), table)
    gre = (ure * bre + uim * bim).astype(bf16)
    gim = (ure * bim - uim * bre).astype(bf16)
    for s in range(PEERS):
        row = ROWS * (s // 4)
        part = gre if row < 64 else gim
        out[SHARES.index(s)] = part[row % 64 : row % 64 + ROWS, 128 * (s % 4) : 128 * (s % 4) + 128]


def share_body(arrived, out):
    total = jnp.zeros((ROWS, 128), f32)
    for s in range(PEERS):
        total = total + arrived[s].astype(f32)
    total = total.astype(bf16)
    for d in range(2 * PEERS):
        out[d] = total


def update_body(shares, contrast, wave, table, updated, out):
    freqs = 2.0 * PEERS
    rows = []
    for group in range(4):
        lanes = []
        for s in range(4 * group, 4 * group + 4):
            z = s // 2
            core = s % 2
            pair = [shares[FREQS.index(4 * z + 2 * y + core)].astype(f32) for y in range(2)]
            lanes.append(pair[0] + pair[1])
        total = jnp.concatenate(lanes, axis=1)
        new = contrast[ROWS * group : ROWS * group + ROWS] - total / freqs
        updated[group // 2, :, group % 2, :] = new
        rows.append(new)
    cre = jnp.concatenate(rows[0:2], axis=0)
    cim = jnp.concatenate(rows[2:4], axis=0)
    vre, vim = times(cre, cim, wave[0:64], wave[64:128])
    wre, wim = fwd_lines(vre, vim, table)
    store_tiles(out, wre, wim)


TILES = ((PEERS, ROWS, 128), bf16)
LINES = ((128, GRID), f32)
IN_VMEM = pl.BlockSpec(memory_space=pltpu.VMEM)
IN_SMEM = pl.BlockSpec(memory_space=pltpu.SMEM)


IN_HBM = pl.BlockSpec(memory_space=pltpu.HBM)


def run(body, outs, *args, spaces=(), scratch=()):
    many = isinstance(outs, list)
    shapes = [jax.ShapeDtypeStruct(*o) for o in (outs if many else [outs])]
    spaces = list(spaces) + [IN_VMEM] * (len(args) - len(spaces))
    return pl.pallas_call(
        body,
        out_shape=shapes if many else shapes[0],
        in_specs=spaces,
        out_specs=[IN_VMEM] * len(shapes) if many else IN_VMEM,
        scratch_shapes=scratch,
        compiler_params=pltpu.CompilerParams(vmem_limit_bytes=40 * 1024 * 1024),
    )(*args)


def stay(array):
    return pltpu.with_memory_space_constraint(array, pltpu.HBM)


def exchange(blocks, axis, groups):
    return lax.all_to_all(
        blocks, axis, split_axis=0, concat_axis=0, tiled=True, axis_index_groups=groups
    )


def local(contrast, green_kernel, source_pos, receiver_pos, measured):
    table = jnp.asarray(dft_tables())
    kernel = green_kernel[0]
    first = (lax.axis_index("plane") * ROWS).astype(jnp.int32)[None]

    source, spectrum, table, places, observed = run(
        source_body,
        [
            TILES,
            ((128, GRID), bf16),
            (table.shape, bf16),
            (receiver_pos.shape, jnp.int32),
            (measured.shape, f32),
        ],
        stay(source_pos),
        first,
        stay(kernel),
        stay(table),
        stay(receiver_pos),
        stay(measured),
        spaces=(IN_HBM, IN_SMEM, IN_HBM, IN_HBM, IN_HBM, IN_HBM),
        scratch=[
            pltpu.VMEM((2, 2, ROWS, GRID), bf16),
            pltpu.SMEM((1, 2), jnp.int32),
            pltpu.SemaphoreType.DMA((7,)),
        ],
    )
    arrived = exchange(source, "plane", [list(ORDER)])
    incident, lines, sent = run(first_line_body, [LINES, LINES, TILES], arrived, contrast, table)
    arrived = exchange(sent, "plane", [list(ORDER)])
    sent = run(spectral_body, TILES, arrived, kernel, table)
    arrived = exchange(sent, "plane", [list(ORDER)])
    sent = run(line_body, TILES, arrived, lines, incident, table)
    arrived = exchange(sent, "plane", [list(ORDER)])
    sent, along_x, along_y = run(
        sampled_body,
        [
            ((PEERS, ROWS + 8, 128), bf16),
            ((2, GRID, RECV), bf16),
            ((2, ROWS, RECV), f32),
        ],
        first,
        arrived,
        kernel,
        table,
        spectrum,
        places,
        spaces=(IN_SMEM,),
    )
    field = exchange(sent, "plane", [list(ORDER)])
    sent = run(back_body, TILES, field, kernel, table, observed, along_x, along_y)
    arrived = exchange(sent, "plane", [list(ORDER)])
    wave, sent = run(gradient_body, [LINES, TILES], arrived, field, incident, table)
    arrived = exchange(sent, "freq", [[4 * (s // 2) + 2 * y + s % 2 for s in SHARES] for y in range(2)])
    sent = run(share_body, ((2 * PEERS, ROWS, 128), bf16), arrived)
    arrived = exchange(sent, "freq", [list(FREQS)])
    updated, sent = run(
        update_body, [(contrast.shape, f32), TILES], arrived, lines, wave, table
    )
    arrived = exchange(sent, "plane", [list(ORDER)])
    sent = run(spectral_body, TILES, arrived, kernel, table)
    arrived = exchange(sent, "plane", [list(ORDER)])
    field = run(field_body, ((1,) + contrast.shape, f32), arrived, incident, table)
    return updated, field


def solution(mesh):
    return jax.shard_map(
        local,
        mesh=mesh,
        in_specs=(
            P(None, "plane", None, None),
            P("freq", None, None, None, "plane", None),
            P("freq", None),
            P("freq", None, None),
            P("freq", None, None),
        ),
        out_specs=(P(None, "plane", None, None), P("freq", None, "plane", None, None)),
        check_vma=False,
    )
```

```python
import math

import jax
import jax.numpy as jnp
import ml_dtypes
import numpy as np
from jax import lax
from jax.experimental import pallas as pl
from jax.experimental.pallas import tpu as pltpu
from jax.sharding import PartitionSpec as P

GRID = 512
ROWS = 32
PEERS = 16
RECV = 64
GAIN = 3.0
f32 = jnp.float32
bf16 = jnp.bfloat16

ORDER = (4, 8, 5, 9, 7, 11, 6, 10, 0, 12, 1, 13, 3, 15, 2, 14)
AT = tuple(ORDER.index(b) for b in range(PEERS))
SHARES = tuple(2 * z + c for z in (0, 1, 7, 2, 6, 3, 5, 4) for c in (1, 0))

FREQS = tuple(4 * z + 2 * y + c for z in (0, 4, 1, 5, 2, 6, 3, 7) for c in (1, 0) for y in (0, 1))


def dft_tables():
    k = np.arange(GRID, dtype=np.int64)
    angle = ((k[:, None] * k[None, :]) % GRID).astype(np.float32) * np.float32(2.0 * math.pi / GRID)
    scale = np.float32(1.0 / math.sqrt(GRID))
    both = np.stack([np.cos(angle) * scale, np.sin(angle) * scale])
    return both.astype(ml_dtypes.bfloat16)


def mm(a, b):
    return jnp.dot(a, b, preferred_element_type=f32)


def mm_nt(a, b):
    return lax.dot_general(a, b, (((1,), (1,)), ((), ())), preferred_element_type=f32)


def swap_groups(x):
    lane = lax.broadcasted_iota(jnp.int32, x[0].shape, 1)
    low = lane < 64
    even = (lane & 32) == 0
    a0 = jnp.where(low, x[0], pltpu.roll(x[2], 64, 1))
    a2 = jnp.where(low, pltpu.roll(x[0], 64, 1), x[2])
    a1 = jnp.where(low, x[1], pltpu.roll(x[3], 64, 1))
    a3 = jnp.where(low, pltpu.roll(x[1], 64, 1), x[3])
    y0 = jnp.where(even, a0, pltpu.roll(a1, 32, 1))
    y1 = jnp.where(even, pltpu.roll(a0, 96, 1), a1)
    y2 = jnp.where(even, a2, pltpu.roll(a3, 32, 1))
    y3 = jnp.where(even, pltpu.roll(a2, 96, 1), a3)
    return [y0, y1, y2, y3]


def lines_of(tiles):
    parts = [[], [], [], []]
    for g in range(4):
        swapped = swap_groups([tiles[AT[4 * g + i], 0:ROWS, :].astype(f32) for i in range(4)])
        for j in range(4):
            parts[j].append(swapped[j])
    return jnp.concatenate([jnp.concatenate(p, axis=1) for p in parts], axis=0).astype(bf16)


def store_tiles(out, re, im):
    quarter = [re[0:ROWS], re[ROWS:], im[0:ROWS], im[ROWS:]]
    for g in range(4):
        swapped = swap_groups([q[:, 128 * g : 128 * g + 128] for q in quarter])
        for j in range(4):
            out[AT[4 * g + j]] = swapped[j].astype(bf16)


def inv_lines(lines, table):
    a = mm(lines, table[0])
    b = mm(lines, table[1])
    return a[0:64] - b[64:128], a[64:128] + b[0:64]


def fwd_lines(re, im, table):
    both = jnp.concatenate([re, im], axis=0).astype(bf16)
    a = mm(both, table[0])
    b = mm(both, table[1])
    return a[0:64] + b[64:128], a[64:128] - b[0:64]


def times(cre, cim, ure, uim):
    return cre * ure - cim * uim, cre * uim + cim * ure


def inv_spectrum(hre, him, table):
    straight = jnp.concatenate([hre, him], axis=0).astype(bf16)
    crossed = jnp.concatenate([-him, hre], axis=0).astype(bf16)
    return mm_nt(table[0], straight) + mm_nt(table[1], crossed)


def store_blocks(out, field):
    field = field.astype(bf16)
    for d in range(PEERS):
        out[AT[d], 0:ROWS, :] = field[ROWS * d : ROWS * d + ROWS]


def couple(kernel, fre, fim):
    hre = []
    him = []
    for lo in range(2):
        sre = None
        sim = None
        for li in range(2):
            kre = kernel[0, lo, li].astype(f32)
            kim = kernel[1, lo, li].astype(f32)
            vre = fre[ROWS * li : ROWS * li + ROWS]
            vim = fim[ROWS * li : ROWS * li + ROWS]
            pre, pim = times(kre, kim, vre, vim)
            sre = pre if sre is None else sre + pre
            sim = pim if sim is None else sim + pim
        hre.append(sre)
        him.append(sim)
    return jnp.concatenate(hre, axis=0), jnp.concatenate(him, axis=0)


def source_body(
    spot_hbm,
    first,
    kernel_hbm,
    table_hbm,
    places_hbm,
    measured_hbm,
    out,
    spectrum,
    table,
    places,
    measured,
    kernel,
    spot,
    sems,
):
    copies = []
    where = pltpu.make_async_copy(spot_hbm, spot, sems.at[4])
    where.start()
    for part in range(2):
        copies.append(
            pltpu.make_async_copy(
                kernel_hbm.at[part, :, 0], kernel.at[part], sems.at[part]
            )
        )
        copies.append(
            pltpu.make_async_copy(table_hbm.at[part], table.at[part], sems.at[2 + part])
        )
    for copy in (copies[0], copies[2], copies[1], copies[3]):
        copy.start()
    extra = [
        pltpu.make_async_copy(places_hbm, places, sems.at[5]),
        pltpu.make_async_copy(measured_hbm, measured, sems.at[6]),
    ]
    for copy in extra:
        copy.start()
    where.wait()
    x0 = spot[0, 0]
    y0 = spot[0, 1]
    step = 2.0 * math.pi / GRID
    kx = lax.broadcasted_iota(jnp.int32, (8, GRID), 1)
    ax = ((kx * x0) & (GRID - 1)).astype(f32) * step
    ky = lax.broadcasted_iota(jnp.int32, (ROWS, 128), 0) + first[0]
    ay = ((ky * y0) & (GRID - 1)).astype(f32) * step
    xre = jnp.cos(ax)[0:1]
    xim = -jnp.sin(ax)[0:1]
    yre = jnp.cos(ay)[:, 0:1]
    yim = -jnp.sin(ay)[:, 0:1]
    qre = GAIN * (yre * xre - yim * xim)
    qim = GAIN * (yre * xim + yim * xre)
    copies[0].wait()
    copies[2].wait()
    zre = []
    zim = []
    for lo in range(2):
        a, b = times(kernel[0, lo].astype(f32), kernel[1, lo].astype(f32), qre, qim)
        zre.append(a)
        zim.append(b)
    zre = jnp.concatenate(zre, axis=0)
    zim = jnp.concatenate(zim, axis=0)
    straight = jnp.concatenate([zre, zim], axis=0).astype(bf16)
    crossed = jnp.concatenate([-zim, zre], axis=0).astype(bf16)
    spectrum[...] = straight
    copies[1].wait()
    field = mm_nt(table[0], straight)
    copies[3].wait()
    field = field + mm_nt(table[1], crossed)
    store_blocks(out, field)
    for copy in extra:
        copy.wait()


def by_part_layer(field, part):
    return jnp.concatenate([field[part, :, 0, :], field[part, :, 1, :]], axis=0)


def first_line_body(tiles, contrast, table, incident, lines, out):
    ure, uim = inv_lines(lines_of(tiles), table)
    incident[0:64] = ure
    incident[64:128] = uim
    cre = by_part_layer(contrast, 0)
    cim = by_part_layer(contrast, 1)
    lines[0:64] = cre
    lines[64:128] = cim
    vre, vim = times(cre, cim, ure, uim)
    wre, wim = fwd_lines(vre, vim, table)
    store_tiles(out, wre, wim)


def line_body(tiles, contrast, incident, table, out):
    dre, dim = inv_lines(lines_of(tiles), table)
    ure = incident[0:64] + dre
    uim = incident[64:128] + dim
    vre, vim = times(contrast[0:64], contrast[64:128], ure, uim)
    wre, wim = fwd_lines(vre, vim, table)
    store_tiles(out, wre, wim)


def coupled(tiles, kernel, table):
    stacked = jnp.concatenate([tiles[AT[d]] for d in range(PEERS)], axis=0)
    turned = stacked.T
    a = mm(turned, table[0])
    b = mm(turned, table[1])
    fre = a[0:64] + b[64:128]
    fim = a[64:128] - b[0:64]
    return couple(kernel, fre, fim)


def spectral_body(tiles, kernel, table, out):
    hre, him = coupled(tiles, kernel, table)
    field = inv_spectrum(hre, him, table)
    store_blocks(out, field)


def last_spectral_body(tiles, kernel, table, updated, out, updated_hbm, sem):
    copy = pltpu.make_async_copy(updated, updated_hbm, sem)
    copy.start()
    spectral_body(tiles, kernel, table, out)
    copy.wait()


def sampled_body(first, tiles, kernel, table, spectrum, places, out, along_x, along_y):
    where = lax.broadcasted_iota(jnp.int32, (GRID, RECV), 0)
    at_x = jnp.where(where == places[0, 0:1, :], 1.0, 0.0).astype(bf16)
    at_y = jnp.where(where == places[0, 1:2, :], 1.0, 0.0).astype(bf16)
    start = pl.multiple_of(first[0], ROWS)
    xre = mm(table[0], at_x).astype(bf16)
    xim = mm(table[1], at_x).astype(bf16)
    yre = mm(table[0, pl.ds(start, ROWS), :], at_y)
    yim = mm(table[1, pl.ds(start, ROWS), :], at_y)
    along_x[0] = xre
    along_x[1] = xim
    along_y[0] = yre
    along_y[1] = yim
    hre, him = coupled(tiles, kernel, table)
    field = inv_spectrum(hre, him, table)
    store_blocks(out, field)
    top = jnp.concatenate([hre[0:ROWS], him[0:ROWS]], axis=0).astype(bf16)
    top = jnp.concatenate([top, spectrum[0:ROWS], spectrum[64 : 64 + ROWS]], axis=0)
    a = mm(top, xre)
    b = mm(top, xim)
    a = a[0:64] + a[64:128]
    b = b[0:64] + b[64:128]
    pre = a[0:ROWS] - b[ROWS:64]
    pim = a[ROWS:64] + b[0:ROWS]
    sre = jnp.sum(pre * yre - pim * yim, axis=0, keepdims=True)
    sim = jnp.sum(pre * yim + pim * yre, axis=0, keepdims=True)
    total = jnp.concatenate([sre, sim], axis=1)
    high = total.astype(bf16).astype(f32)
    low = total - high
    row = lax.broadcasted_iota(jnp.int32, (8, 128), 0)
    extra = jnp.where(row == 0, high, jnp.where(row == 1, low, 0.0)).astype(bf16)
    for d in range(PEERS):
        out[d, ROWS : ROWS + 8, :] = extra


def back_body(tiles, kernel, table, measured, along_x, along_y, out):
    sums = jnp.zeros((8, 128), f32)
    for s in range(PEERS):
        sums = sums + tiles[s, ROWS : ROWS + 8, :].astype(f32)
    sums = sums[0:1] + sums[1:2]
    mre = sums[:, 0:RECV] - measured[0, 0:1, :]
    mim = sums[:, RECV : 2 * RECV] - measured[0, 1:2, :]
    yre = along_y[0]
    yim = along_y[1]
    mixed_re = mre * yre + mim * yim
    mixed_im = mim * yre - mre * yim
    mixed = jnp.concatenate([mixed_re, mixed_im], axis=0).astype(bf16)
    a = mm_nt(mixed, along_x[0])
    b = mm_nt(mixed, along_x[1])
    bre = (a[0:ROWS] + b[ROWS : 2 * ROWS]) * float(GRID)
    bim = (a[ROWS : 2 * ROWS] - b[0:ROWS]) * float(GRID)
    hre = []
    him = []
    for l in range(2):
        kre = kernel[0, 0, l].astype(f32)
        kim = kernel[1, 0, l].astype(f32)
        hre.append(kre * bre + kim * bim)
        him.append(kre * bim - kim * bre)
    field = inv_spectrum(jnp.concatenate(hre, axis=0), jnp.concatenate(him, axis=0), table)
    store_blocks(out, field)


def field_body(tiles, incident, table, out):
    dre, dim = inv_lines(lines_of(tiles), table)
    for part, delta in enumerate((dre, dim)):
        total = incident[64 * part : 64 * part + 64] + delta
        for l in range(2):
            out[0, part, :, l, :] = total[ROWS * l : ROWS * l + ROWS]


def gradient_body(tiles, field_tiles, incident, table, wave, out):
    dre, dim = inv_lines(lines_of(field_tiles), table)
    ure = incident[0:64] + dre
    uim = incident[64:128] + dim
    wave[0:64] = ure
    wave[64:128] = uim
    bre, bim = inv_lines(lines_of(tiles), table)
    gre = (ure * bre + uim * bim).astype(bf16)
    gim = (ure * bim - uim * bre).astype(bf16)
    for s in range(PEERS):
        row = ROWS * (s // 4)
        part = gre if row < 64 else gim
        out[SHARES.index(s)] = part[row % 64 : row % 64 + ROWS, 128 * (s % 4) : 128 * (s % 4) + 128]


def share_body(arrived, out):
    total = jnp.zeros((ROWS, 128), f32)
    for s in range(PEERS):
        total = total + arrived[s].astype(f32)
    total = total.astype(bf16)
    for d in range(2 * PEERS):
        out[d] = total


def update_body(shares, contrast, wave, table, updated, out):
    freqs = 2.0 * PEERS
    rows = []
    for group in range(4):
        lanes = []
        for s in range(4 * group, 4 * group + 4):
            z = s // 2
            core = s % 2
            pair = [shares[FREQS.index(4 * z + 2 * y + core)].astype(f32) for y in range(2)]
            lanes.append(pair[0] + pair[1])
        total = jnp.concatenate(lanes, axis=1)
        new = contrast[ROWS * group : ROWS * group + ROWS] - total / freqs
        updated[group // 2, :, group % 2, :] = new
        rows.append(new)
    cre = jnp.concatenate(rows[0:2], axis=0)
    cim = jnp.concatenate(rows[2:4], axis=0)
    vre, vim = times(cre, cim, wave[0:64], wave[64:128])
    wre, wim = fwd_lines(vre, vim, table)
    store_tiles(out, wre, wim)


TILES = ((PEERS, ROWS, 128), bf16)
LINES = ((128, GRID), f32)
IN_VMEM = pl.BlockSpec(memory_space=pltpu.VMEM)
IN_SMEM = pl.BlockSpec(memory_space=pltpu.SMEM)


IN_HBM = pl.BlockSpec(memory_space=pltpu.HBM)


def run(body, outs, *args, spaces=(), scratch=(), places=None):
    many = isinstance(outs, list)
    shapes = [jax.ShapeDtypeStruct(*o) for o in (outs if many else [outs])]
    spaces = list(spaces) + [IN_VMEM] * (len(args) - len(spaces))
    return pl.pallas_call(
        body,
        out_shape=shapes if many else shapes[0],
        in_specs=spaces,
        out_specs=places or ([IN_VMEM] * len(shapes) if many else IN_VMEM),
        scratch_shapes=scratch,
        compiler_params=pltpu.CompilerParams(vmem_limit_bytes=40 * 1024 * 1024),
    )(*args)


def stay(array):
    return pltpu.with_memory_space_constraint(array, pltpu.HBM)


def exchange(blocks, axis, groups):
    return lax.all_to_all(
        blocks, axis, split_axis=0, concat_axis=0, tiled=True, axis_index_groups=groups
    )


def local(contrast, green_kernel, source_pos, receiver_pos, measured):
    table = jnp.asarray(dft_tables())
    kernel = green_kernel[0]
    first = (lax.axis_index("plane") * ROWS).astype(jnp.int32)[None]

    source, spectrum, table, places, observed = run(
        source_body,
        [
            TILES,
            ((128, GRID), bf16),
            (table.shape, bf16),
            (receiver_pos.shape, jnp.int32),
            (measured.shape, f32),
        ],
        stay(source_pos),
        first,
        stay(kernel),
        stay(table),
        stay(receiver_pos),
        stay(measured),
        spaces=(IN_HBM, IN_SMEM, IN_HBM, IN_HBM, IN_HBM, IN_HBM),
        scratch=[
            pltpu.VMEM((2, 2, ROWS, GRID), bf16),
            pltpu.SMEM((1, 2), jnp.int32),
            pltpu.SemaphoreType.DMA((7,)),
        ],
    )
    arrived = exchange(source, "plane", [list(ORDER)])
    incident, lines, sent = run(first_line_body, [LINES, LINES, TILES], arrived, contrast, table)
    arrived = exchange(sent, "plane", [list(ORDER)])
    sent = run(spectral_body, TILES, arrived, kernel, table)
    arrived = exchange(sent, "plane", [list(ORDER)])
    sent = run(line_body, TILES, arrived, lines, incident, table)
    arrived = exchange(sent, "plane", [list(ORDER)])
    sent, along_x, along_y = run(
        sampled_body,
        [
            ((PEERS, ROWS + 8, 128), bf16),
            ((2, GRID, RECV), bf16),
            ((2, ROWS, RECV), f32),
        ],
        first,
        arrived,
        kernel,
        table,
        spectrum,
        places,
        spaces=(IN_SMEM,),
    )
    field = exchange(sent, "plane", [list(ORDER)])
    sent = run(back_body, TILES, field, kernel, table, observed, along_x, along_y)
    arrived = exchange(sent, "plane", [list(ORDER)])
    wave, sent = run(gradient_body, [LINES, TILES], arrived, field, incident, table)
    arrived = exchange(sent, "freq", [[4 * (s // 2) + 2 * y + s % 2 for s in SHARES] for y in range(2)])
    sent = run(share_body, ((2 * PEERS, ROWS, 128), bf16), arrived)
    arrived = exchange(sent, "freq", [list(FREQS)])
    updated, sent = run(
        update_body, [(contrast.shape, f32), TILES], arrived, lines, wave, table
    )
    arrived = exchange(sent, "plane", [list(ORDER)])
    sent, updated = run(
        last_spectral_body,
        [TILES, (contrast.shape, f32)],
        arrived,
        kernel,
        table,
        updated,
        scratch=[pltpu.SemaphoreType.DMA],
        places=[IN_VMEM, IN_HBM],
    )
    arrived = exchange(sent, "plane", [list(ORDER)])
    field = run(field_body, ((1,) + contrast.shape, f32), arrived, incident, table)
    return updated, field


def solution(mesh):
    return jax.shard_map(
        local,
        mesh=mesh,
        in_specs=(
            P(None, "plane", None, None),
            P("freq", None, None, None, "plane", None),
            P("freq", None),
            P("freq", None, None),
            P("freq", None, None),
        ),
        out_specs=(P(None, "plane", None, None), P("freq", None, "plane", None, None)),
        check_vma=False,
    )
```

```python
import math

import jax
import jax.numpy as jnp
import ml_dtypes
import numpy as np
from jax import lax
from jax.experimental import pallas as pl
from jax.experimental.pallas import tpu as pltpu
from jax.sharding import PartitionSpec as P

GRID = 512
ROWS = 32
PEERS = 16
RECV = 64
GAIN = 3.0
f32 = jnp.float32
bf16 = jnp.bfloat16

ORDER = (5, 12, 4, 3, 1, 13, 7, 0, 9, 2, 6, 11, 8, 15, 14, 10)
AT = tuple(ORDER.index(b) for b in range(PEERS))
SHARES = tuple(2 * z + c for z in (0, 1, 7, 2, 6, 3, 5, 4) for c in (1, 0))

FREQS = tuple(4 * z + 2 * y + c for z in (0, 4, 1, 5, 2, 6, 3, 7) for c in (1, 0) for y in (0, 1))


def dft_tables():
    k = np.arange(GRID, dtype=np.int64)
    angle = ((k[:, None] * k[None, :]) % GRID).astype(np.float32) * np.float32(2.0 * math.pi / GRID)
    scale = np.float32(1.0 / math.sqrt(GRID))
    both = np.stack([np.cos(angle) * scale, np.sin(angle) * scale])
    return both.astype(ml_dtypes.bfloat16)


def mm(a, b):
    return jnp.dot(a, b, preferred_element_type=f32)


def mm_nt(a, b):
    return lax.dot_general(a, b, (((1,), (1,)), ((), ())), preferred_element_type=f32)


def swap_groups(x):
    lane = lax.broadcasted_iota(jnp.int32, x[0].shape, 1)
    low = lane < 64
    even = (lane & 32) == 0
    a0 = jnp.where(low, x[0], pltpu.roll(x[2], 64, 1))
    a2 = jnp.where(low, pltpu.roll(x[0], 64, 1), x[2])
    a1 = jnp.where(low, x[1], pltpu.roll(x[3], 64, 1))
    a3 = jnp.where(low, pltpu.roll(x[1], 64, 1), x[3])
    y0 = jnp.where(even, a0, pltpu.roll(a1, 32, 1))
    y1 = jnp.where(even, pltpu.roll(a0, 96, 1), a1)
    y2 = jnp.where(even, a2, pltpu.roll(a3, 32, 1))
    y3 = jnp.where(even, pltpu.roll(a2, 96, 1), a3)
    return [y0, y1, y2, y3]


def lines_of(tiles):
    parts = [[], [], [], []]
    for g in range(4):
        swapped = swap_groups([tiles[AT[4 * g + i], 0:ROWS, :].astype(f32) for i in range(4)])
        for j in range(4):
            parts[j].append(swapped[j])
    return jnp.concatenate([jnp.concatenate(p, axis=1) for p in parts], axis=0).astype(bf16)


def store_tiles(out, re, im):
    quarter = [re[0:ROWS], re[ROWS:], im[0:ROWS], im[ROWS:]]
    for g in range(4):
        swapped = swap_groups([q[:, 128 * g : 128 * g + 128] for q in quarter])
        for j in range(4):
            out[AT[4 * g + j]] = swapped[j].astype(bf16)


def inv_lines(lines, table):
    a = mm(lines, table[0])
    b = mm(lines, table[1])
    return a[0:64] - b[64:128], a[64:128] + b[0:64]


def fwd_lines(re, im, table):
    both = jnp.concatenate([re, im], axis=0).astype(bf16)
    a = mm(both, table[0])
    b = mm(both, table[1])
    return a[0:64] + b[64:128], a[64:128] - b[0:64]


def times(cre, cim, ure, uim):
    return cre * ure - cim * uim, cre * uim + cim * ure


def inv_spectrum(hre, him, table):
    straight = jnp.concatenate([hre, him], axis=0).astype(bf16)
    crossed = jnp.concatenate([-him, hre], axis=0).astype(bf16)
    return mm_nt(table[0], straight) + mm_nt(table[1], crossed)


def store_blocks(out, field):
    field = field.astype(bf16)
    for d in range(PEERS):
        out[AT[d], 0:ROWS, :] = field[ROWS * d : ROWS * d + ROWS]


def couple(kernel, fre, fim):
    hre = []
    him = []
    for lo in range(2):
        sre = None
        sim = None
        for li in range(2):
            kre = kernel[0, lo, li].astype(f32)
            kim = kernel[1, lo, li].astype(f32)
            vre = fre[ROWS * li : ROWS * li + ROWS]
            vim = fim[ROWS * li : ROWS * li + ROWS]
            pre, pim = times(kre, kim, vre, vim)
            sre = pre if sre is None else sre + pre
            sim = pim if sim is None else sim + pim
        hre.append(sre)
        him.append(sim)
    return jnp.concatenate(hre, axis=0), jnp.concatenate(him, axis=0)


def source_body(
    spot_hbm,
    first,
    kernel_hbm,
    table_hbm,
    places_hbm,
    measured_hbm,
    out,
    spectrum,
    table,
    places,
    measured,
    kernel,
    spot,
    sems,
):
    copies = []
    where = pltpu.make_async_copy(spot_hbm, spot, sems.at[4])
    where.start()
    for part in range(2):
        copies.append(
            pltpu.make_async_copy(
                kernel_hbm.at[part, :, 0], kernel.at[part], sems.at[part]
            )
        )
        copies.append(
            pltpu.make_async_copy(table_hbm.at[part], table.at[part], sems.at[2 + part])
        )
    for copy in (copies[0], copies[2], copies[1], copies[3]):
        copy.start()
    extra = [
        pltpu.make_async_copy(places_hbm, places, sems.at[5]),
        pltpu.make_async_copy(measured_hbm, measured, sems.at[6]),
    ]
    for copy in extra:
        copy.start()
    where.wait()
    x0 = spot[0, 0]
    y0 = spot[0, 1]
    step = 2.0 * math.pi / GRID
    kx = lax.broadcasted_iota(jnp.int32, (8, GRID), 1)
    ax = ((kx * x0) & (GRID - 1)).astype(f32) * step
    ky = lax.broadcasted_iota(jnp.int32, (ROWS, 128), 0) + first[0]
    ay = ((ky * y0) & (GRID - 1)).astype(f32) * step
    xre = jnp.cos(ax)[0:1]
    xim = -jnp.sin(ax)[0:1]
    yre = jnp.cos(ay)[:, 0:1]
    yim = -jnp.sin(ay)[:, 0:1]
    qre = GAIN * (yre * xre - yim * xim)
    qim = GAIN * (yre * xim + yim * xre)
    copies[0].wait()
    copies[2].wait()
    zre = []
    zim = []
    for lo in range(2):
        a, b = times(kernel[0, lo].astype(f32), kernel[1, lo].astype(f32), qre, qim)
        zre.append(a)
        zim.append(b)
    zre = jnp.concatenate(zre, axis=0)
    zim = jnp.concatenate(zim, axis=0)
    straight = jnp.concatenate([zre, zim], axis=0).astype(bf16)
    crossed = jnp.concatenate([-zim, zre], axis=0).astype(bf16)
    spectrum[...] = straight
    copies[1].wait()
    field = mm_nt(table[0], straight)
    copies[3].wait()
    field = field + mm_nt(table[1], crossed)
    store_blocks(out, field)
    for copy in extra:
        copy.wait()


def by_part_layer(field, part):
    return jnp.concatenate([field[part, :, 0, :], field[part, :, 1, :]], axis=0)


def first_line_body(tiles, contrast, table, incident, lines, out):
    ure, uim = inv_lines(lines_of(tiles), table)
    incident[0:64] = ure
    incident[64:128] = uim
    cre = by_part_layer(contrast, 0)
    cim = by_part_layer(contrast, 1)
    lines[0:64] = cre
    lines[64:128] = cim
    vre, vim = times(cre, cim, ure, uim)
    wre, wim = fwd_lines(vre, vim, table)
    store_tiles(out, wre, wim)


def line_body(tiles, contrast, incident, table, out):
    dre, dim = inv_lines(lines_of(tiles), table)
    ure = incident[0:64] + dre
    uim = incident[64:128] + dim
    vre, vim = times(contrast[0:64], contrast[64:128], ure, uim)
    wre, wim = fwd_lines(vre, vim, table)
    store_tiles(out, wre, wim)


def coupled(tiles, kernel, table):
    stacked = jnp.concatenate([tiles[AT[d]] for d in range(PEERS)], axis=0)
    turned = stacked.T
    a = mm(turned, table[0])
    b = mm(turned, table[1])
    fre = a[0:64] + b[64:128]
    fim = a[64:128] - b[0:64]
    return couple(kernel, fre, fim)


def spectral_body(tiles, kernel, table, out):
    hre, him = coupled(tiles, kernel, table)
    field = inv_spectrum(hre, him, table)
    store_blocks(out, field)


def last_spectral_body(tiles, kernel, table, updated, out, updated_hbm, sem):
    copy = pltpu.make_async_copy(updated, updated_hbm, sem)
    copy.start()
    spectral_body(tiles, kernel, table, out)
    copy.wait()


def sampled_body(first, tiles, kernel, table, spectrum, places, out, along_x, along_y):
    where = lax.broadcasted_iota(jnp.int32, (GRID, RECV), 0)
    at_x = jnp.where(where == places[0, 0:1, :], 1.0, 0.0).astype(bf16)
    at_y = jnp.where(where == places[0, 1:2, :], 1.0, 0.0).astype(bf16)
    start = pl.multiple_of(first[0], ROWS)
    xre = mm(table[0], at_x).astype(bf16)
    xim = mm(table[1], at_x).astype(bf16)
    yre = mm(table[0, pl.ds(start, ROWS), :], at_y)
    yim = mm(table[1, pl.ds(start, ROWS), :], at_y)
    along_x[0] = xre
    along_x[1] = xim
    along_y[0] = yre
    along_y[1] = yim
    hre, him = coupled(tiles, kernel, table)
    field = inv_spectrum(hre, him, table)
    store_blocks(out, field)
    top = jnp.concatenate([hre[0:ROWS], him[0:ROWS]], axis=0).astype(bf16)
    top = jnp.concatenate([top, spectrum[0:ROWS], spectrum[64 : 64 + ROWS]], axis=0)
    a = mm(top, xre)
    b = mm(top, xim)
    a = a[0:64] + a[64:128]
    b = b[0:64] + b[64:128]
    pre = a[0:ROWS] - b[ROWS:64]
    pim = a[ROWS:64] + b[0:ROWS]
    sre = jnp.sum(pre * yre - pim * yim, axis=0, keepdims=True)
    sim = jnp.sum(pre * yim + pim * yre, axis=0, keepdims=True)
    total = jnp.concatenate([sre, sim], axis=1)
    high = total.astype(bf16).astype(f32)
    low = total - high
    row = lax.broadcasted_iota(jnp.int32, (8, 128), 0)
    extra = jnp.where(row == 0, high, jnp.where(row == 1, low, 0.0)).astype(bf16)
    for d in range(PEERS):
        out[d, ROWS : ROWS + 8, :] = extra


def back_body(tiles, kernel, table, measured, along_x, along_y, out):
    sums = jnp.zeros((8, 128), f32)
    for s in range(PEERS):
        sums = sums + tiles[s, ROWS : ROWS + 8, :].astype(f32)
    sums = sums[0:1] + sums[1:2]
    mre = sums[:, 0:RECV] - measured[0, 0:1, :]
    mim = sums[:, RECV : 2 * RECV] - measured[0, 1:2, :]
    yre = along_y[0]
    yim = along_y[1]
    mixed_re = mre * yre + mim * yim
    mixed_im = mim * yre - mre * yim
    mixed = jnp.concatenate([mixed_re, mixed_im], axis=0).astype(bf16)
    a = mm_nt(mixed, along_x[0])
    b = mm_nt(mixed, along_x[1])
    bre = (a[0:ROWS] + b[ROWS : 2 * ROWS]) * float(GRID)
    bim = (a[ROWS : 2 * ROWS] - b[0:ROWS]) * float(GRID)
    hre = []
    him = []
    for l in range(2):
        kre = kernel[0, 0, l].astype(f32)
        kim = kernel[1, 0, l].astype(f32)
        hre.append(kre * bre + kim * bim)
        him.append(kre * bim - kim * bre)
    field = inv_spectrum(jnp.concatenate(hre, axis=0), jnp.concatenate(him, axis=0), table)
    store_blocks(out, field)


def field_body(tiles, incident, table, out):
    dre, dim = inv_lines(lines_of(tiles), table)
    for part, delta in enumerate((dre, dim)):
        total = incident[64 * part : 64 * part + 64] + delta
        for l in range(2):
            out[0, part, :, l, :] = total[ROWS * l : ROWS * l + ROWS]


def gradient_body(tiles, field_tiles, incident, table, wave, out):
    dre, dim = inv_lines(lines_of(field_tiles), table)
    ure = incident[0:64] + dre
    uim = incident[64:128] + dim
    wave[0:64] = ure
    wave[64:128] = uim
    bre, bim = inv_lines(lines_of(tiles), table)
    gre = (ure * bre + uim * bim).astype(bf16)
    gim = (ure * bim - uim * bre).astype(bf16)
    for s in range(PEERS):
        row = ROWS * (s // 4)
        part = gre if row < 64 else gim
        out[SHARES.index(s)] = part[row % 64 : row % 64 + ROWS, 128 * (s % 4) : 128 * (s % 4) + 128]


def share_body(arrived, out):
    total = jnp.zeros((ROWS, 128), f32)
    for s in range(PEERS):
        total = total + arrived[s].astype(f32)
    total = total.astype(bf16)
    for d in range(2 * PEERS):
        out[d] = total


def update_body(shares, contrast, wave, table, updated, out):
    freqs = 2.0 * PEERS
    rows = []
    for group in range(4):
        lanes = []
        for s in range(4 * group, 4 * group + 4):
            z = s // 2
            core = s % 2
            pair = [shares[FREQS.index(4 * z + 2 * y + core)].astype(f32) for y in range(2)]
            lanes.append(pair[0] + pair[1])
        total = jnp.concatenate(lanes, axis=1)
        new = contrast[ROWS * group : ROWS * group + ROWS] - total / freqs
        updated[group // 2, :, group % 2, :] = new
        rows.append(new)
    cre = jnp.concatenate(rows[0:2], axis=0)
    cim = jnp.concatenate(rows[2:4], axis=0)
    vre, vim = times(cre, cim, wave[0:64], wave[64:128])
    wre, wim = fwd_lines(vre, vim, table)
    store_tiles(out, wre, wim)


TILES = ((PEERS, ROWS, 128), bf16)
LINES = ((128, GRID), f32)
IN_VMEM = pl.BlockSpec(memory_space=pltpu.VMEM)
IN_SMEM = pl.BlockSpec(memory_space=pltpu.SMEM)


IN_HBM = pl.BlockSpec(memory_space=pltpu.HBM)


def run(body, outs, *args, spaces=(), scratch=(), places=None):
    many = isinstance(outs, list)
    shapes = [jax.ShapeDtypeStruct(*o) for o in (outs if many else [outs])]
    spaces = list(spaces) + [IN_VMEM] * (len(args) - len(spaces))
    return pl.pallas_call(
        body,
        out_shape=shapes if many else shapes[0],
        in_specs=spaces,
        out_specs=places or ([IN_VMEM] * len(shapes) if many else IN_VMEM),
        scratch_shapes=scratch,
        compiler_params=pltpu.CompilerParams(vmem_limit_bytes=40 * 1024 * 1024),
    )(*args)


def stay(array):
    return pltpu.with_memory_space_constraint(array, pltpu.HBM)


def exchange(blocks, axis, groups):
    return lax.all_to_all(
        blocks, axis, split_axis=0, concat_axis=0, tiled=True, axis_index_groups=groups
    )


def local(contrast, green_kernel, source_pos, receiver_pos, measured):
    table = jnp.asarray(dft_tables())
    kernel = green_kernel[0]
    first = (lax.axis_index("plane") * ROWS).astype(jnp.int32)[None]

    source, spectrum, table, places, observed = run(
        source_body,
        [
            TILES,
            ((128, GRID), bf16),
            (table.shape, bf16),
            (receiver_pos.shape, jnp.int32),
            (measured.shape, f32),
        ],
        stay(source_pos),
        first,
        stay(kernel),
        stay(table),
        stay(receiver_pos),
        stay(measured),
        spaces=(IN_HBM, IN_SMEM, IN_HBM, IN_HBM, IN_HBM, IN_HBM),
        scratch=[
            pltpu.VMEM((2, 2, ROWS, GRID), bf16),
            pltpu.SMEM((1, 2), jnp.int32),
            pltpu.SemaphoreType.DMA((7,)),
        ],
    )
    arrived = exchange(source, "plane", [list(ORDER)])
    incident, lines, sent = run(first_line_body, [LINES, LINES, TILES], arrived, contrast, table)
    arrived = exchange(sent, "plane", [list(ORDER)])
    sent = run(spectral_body, TILES, arrived, kernel, table)
    arrived = exchange(sent, "plane", [list(ORDER)])
    sent = run(line_body, TILES, arrived, lines, incident, table)
    arrived = exchange(sent, "plane", [list(ORDER)])
    sent, along_x, along_y = run(
        sampled_body,
        [
            ((PEERS, ROWS + 8, 128), bf16),
            ((2, GRID, RECV), bf16),
            ((2, ROWS, RECV), f32),
        ],
        first,
        arrived,
        kernel,
        table,
        spectrum,
        places,
        spaces=(IN_SMEM,),
    )
    field = exchange(sent, "plane", [list(ORDER)])
    sent = run(back_body, TILES, field, kernel, table, observed, along_x, along_y)
    arrived = exchange(sent, "plane", [list(ORDER)])
    wave, sent = run(gradient_body, [LINES, TILES], arrived, field, incident, table)
    arrived = exchange(sent, "freq", [[4 * (s // 2) + 2 * y + s % 2 for s in SHARES] for y in range(2)])
    sent = run(share_body, ((2 * PEERS, ROWS, 128), bf16), arrived)
    arrived = exchange(sent, "freq", [list(FREQS)])
    updated, sent = run(
        update_body, [(contrast.shape, f32), TILES], arrived, lines, wave, table
    )
    arrived = exchange(sent, "plane", [list(ORDER)])
    sent, updated = run(
        last_spectral_body,
        [TILES, (contrast.shape, f32)],
        arrived,
        kernel,
        table,
        updated,
        scratch=[pltpu.SemaphoreType.DMA],
        places=[IN_VMEM, IN_HBM],
    )
    arrived = exchange(sent, "plane", [list(ORDER)])
    field = run(field_body, ((1,) + contrast.shape, f32), arrived, incident, table)
    return updated, field


def solution(mesh):
    return jax.shard_map(
        local,
        mesh=mesh,
        in_specs=(
            P(None, "plane", None, None),
            P("freq", None, None, None, "plane", None),
            P("freq", None),
            P("freq", None, None),
            P("freq", None, None),
        ),
        out_specs=(P(None, "plane", None, None), P("freq", None, "plane", None, None)),
        check_vma=False,
    )
```

```python
import math

import jax
import jax.numpy as jnp
import ml_dtypes
import numpy as np
from jax import lax
from jax.experimental import pallas as pl
from jax.experimental.pallas import tpu as pltpu
from jax.sharding import PartitionSpec as P

GRID = 512
ROWS = 32
PEERS = 16
RECV = 64
GAIN = 3.0
f32 = jnp.float32
bf16 = jnp.bfloat16

ORDER = (5, 12, 4, 3, 1, 13, 7, 0, 9, 2, 6, 11, 8, 15, 14, 10)
AT = tuple(ORDER.index(b) for b in range(PEERS))
SHARES = tuple(2 * z + c for c in (1, 0) for z in range(8))

FREQS = (
    19, 28, 4, 5, 13, 29, 1, 17, 7, 25, 9, 8, 12, 14, 0, 24,
    15, 2, 30, 23, 10, 20, 16, 22, 3, 27, 26, 11, 21, 18, 31, 6,
)


def dft_tables():
    k = np.arange(GRID, dtype=np.int64)
    angle = ((k[:, None] * k[None, :]) % GRID).astype(np.float32) * np.float32(2.0 * math.pi / GRID)
    scale = np.float32(1.0 / math.sqrt(GRID))
    both = np.stack([np.cos(angle) * scale, np.sin(angle) * scale])
    return both.astype(ml_dtypes.bfloat16)


def mm(a, b):
    return jnp.dot(a, b, preferred_element_type=f32)


def mm_nt(a, b):
    return lax.dot_general(a, b, (((1,), (1,)), ((), ())), preferred_element_type=f32)


def swap_groups(x):
    lane = lax.broadcasted_iota(jnp.int32, x[0].shape, 1)
    low = lane < 64
    even = (lane & 32) == 0
    a0 = jnp.where(low, x[0], pltpu.roll(x[2], 64, 1))
    a2 = jnp.where(low, pltpu.roll(x[0], 64, 1), x[2])
    a1 = jnp.where(low, x[1], pltpu.roll(x[3], 64, 1))
    a3 = jnp.where(low, pltpu.roll(x[1], 64, 1), x[3])
    y0 = jnp.where(even, a0, pltpu.roll(a1, 32, 1))
    y1 = jnp.where(even, pltpu.roll(a0, 96, 1), a1)
    y2 = jnp.where(even, a2, pltpu.roll(a3, 32, 1))
    y3 = jnp.where(even, pltpu.roll(a2, 96, 1), a3)
    return [y0, y1, y2, y3]


def lines_of(tiles):
    parts = [[], [], [], []]
    for g in range(4):
        swapped = swap_groups([tiles[AT[4 * g + i], 0:ROWS, :].astype(f32) for i in range(4)])
        for j in range(4):
            parts[j].append(swapped[j])
    return jnp.concatenate([jnp.concatenate(p, axis=1) for p in parts], axis=0).astype(bf16)


def store_tiles(out, re, im):
    quarter = [re[0:ROWS], re[ROWS:], im[0:ROWS], im[ROWS:]]
    for g in range(4):
        swapped = swap_groups([q[:, 128 * g : 128 * g + 128] for q in quarter])
        for j in range(4):
            out[AT[4 * g + j]] = swapped[j].astype(bf16)


def inv_lines(lines, table):
    a = mm(lines, table[0])
    b = mm(lines, table[1])
    return a[0:64] - b[64:128], a[64:128] + b[0:64]


def fwd_lines(re, im, table):
    both = jnp.concatenate([re, im], axis=0).astype(bf16)
    a = mm(both, table[0])
    b = mm(both, table[1])
    return a[0:64] + b[64:128], a[64:128] - b[0:64]


def times(cre, cim, ure, uim):
    return cre * ure - cim * uim, cre * uim + cim * ure


def inv_spectrum(hre, him, table):
    straight = jnp.concatenate([hre, him], axis=0).astype(bf16)
    crossed = jnp.concatenate([-him, hre], axis=0).astype(bf16)
    return mm_nt(table[0], straight) + mm_nt(table[1], crossed)


def store_blocks(out, field):
    field = field.astype(bf16)
    for d in range(PEERS):
        out[AT[d], 0:ROWS, :] = field[ROWS * d : ROWS * d + ROWS]


def couple(kernel, fre, fim):
    hre = []
    him = []
    for lo in range(2):
        sre = None
        sim = None
        for li in range(2):
            kre = kernel[0, lo, li].astype(f32)
            kim = kernel[1, lo, li].astype(f32)
            vre = fre[ROWS * li : ROWS * li + ROWS]
            vim = fim[ROWS * li : ROWS * li + ROWS]
            pre, pim = times(kre, kim, vre, vim)
            sre = pre if sre is None else sre + pre
            sim = pim if sim is None else sim + pim
        hre.append(sre)
        him.append(sim)
    return jnp.concatenate(hre, axis=0), jnp.concatenate(him, axis=0)


def source_body(
    spot_hbm,
    first,
    kernel_hbm,
    table_hbm,
    places_hbm,
    measured_hbm,
    out,
    spectrum,
    table,
    places,
    measured,
    kernel,
    spot,
    sems,
):
    copies = []
    where = pltpu.make_async_copy(spot_hbm, spot, sems.at[4])
    where.start()
    for part in range(2):
        copies.append(
            pltpu.make_async_copy(
                kernel_hbm.at[part, :, 0], kernel.at[part], sems.at[part]
            )
        )
        copies.append(
            pltpu.make_async_copy(table_hbm.at[part], table.at[part], sems.at[2 + part])
        )
    for copy in (copies[0], copies[2], copies[1], copies[3]):
        copy.start()
    extra = [
        pltpu.make_async_copy(places_hbm, places, sems.at[5]),
        pltpu.make_async_copy(measured_hbm, measured, sems.at[6]),
    ]
    for copy in extra:
        copy.start()
    where.wait()
    x0 = spot[0, 0]
    y0 = spot[0, 1]
    step = 2.0 * math.pi / GRID
    kx = lax.broadcasted_iota(jnp.int32, (8, GRID), 1)
    ax = ((kx * x0) & (GRID - 1)).astype(f32) * step
    ky = lax.broadcasted_iota(jnp.int32, (ROWS, 128), 0) + first[0]
    ay = ((ky * y0) & (GRID - 1)).astype(f32) * step
    xre = jnp.cos(ax)[0:1]
    xim = -jnp.sin(ax)[0:1]
    yre = jnp.cos(ay)[:, 0:1]
    yim = -jnp.sin(ay)[:, 0:1]
    qre = GAIN * (yre * xre - yim * xim)
    qim = GAIN * (yre * xim + yim * xre)
    copies[0].wait()
    copies[2].wait()
    zre = []
    zim = []
    for lo in range(2):
        a, b = times(kernel[0, lo].astype(f32), kernel[1, lo].astype(f32), qre, qim)
        zre.append(a)
        zim.append(b)
    zre = jnp.concatenate(zre, axis=0)
    zim = jnp.concatenate(zim, axis=0)
    straight = jnp.concatenate([zre, zim], axis=0).astype(bf16)
    crossed = jnp.concatenate([-zim, zre], axis=0).astype(bf16)
    spectrum[...] = straight
    copies[1].wait()
    field = mm_nt(table[0], straight)
    copies[3].wait()
    field = field + mm_nt(table[1], crossed)
    store_blocks(out, field)
    for copy in extra:
        copy.wait()


def by_part_layer(field, part):
    return jnp.concatenate([field[part, :, 0, :], field[part, :, 1, :]], axis=0)


def first_line_body(tiles, contrast, table, incident, lines, out):
    ure, uim = inv_lines(lines_of(tiles), table)
    incident[0:64] = ure
    incident[64:128] = uim
    cre = by_part_layer(contrast, 0)
    cim = by_part_layer(contrast, 1)
    lines[0:64] = cre
    lines[64:128] = cim
    vre, vim = times(cre, cim, ure, uim)
    wre, wim = fwd_lines(vre, vim, table)
    store_tiles(out, wre, wim)


def line_body(tiles, contrast, incident, table, out):
    dre, dim = inv_lines(lines_of(tiles), table)
    ure = incident[0:64] + dre
    uim = incident[64:128] + dim
    vre, vim = times(contrast[0:64], contrast[64:128], ure, uim)
    wre, wim = fwd_lines(vre, vim, table)
    store_tiles(out, wre, wim)


def coupled(tiles, kernel, table):
    stacked = jnp.concatenate([tiles[AT[d]] for d in range(PEERS)], axis=0)
    turned = stacked.T
    a = mm(turned, table[0])
    b = mm(turned, table[1])
    fre = a[0:64] + b[64:128]
    fim = a[64:128] - b[0:64]
    return couple(kernel, fre, fim)


def spectral_body(tiles, kernel, table, out):
    hre, him = coupled(tiles, kernel, table)
    field = inv_spectrum(hre, him, table)
    store_blocks(out, field)


def last_spectral_body(tiles, kernel, table, updated, out, updated_hbm, sem):
    copy = pltpu.make_async_copy(updated, updated_hbm, sem)
    copy.start()
    spectral_body(tiles, kernel, table, out)
    copy.wait()


def sampled_body(first, tiles, kernel, table, spectrum, places, out, along_x, along_y):
    where = lax.broadcasted_iota(jnp.int32, (GRID, RECV), 0)
    at_x = jnp.where(where == places[0, 0:1, :], 1.0, 0.0).astype(bf16)
    at_y = jnp.where(where == places[0, 1:2, :], 1.0, 0.0).astype(bf16)
    start = pl.multiple_of(first[0], ROWS)
    xre = mm(table[0], at_x).astype(bf16)
    xim = mm(table[1], at_x).astype(bf16)
    yre = mm(table[0, pl.ds(start, ROWS), :], at_y)
    yim = mm(table[1, pl.ds(start, ROWS), :], at_y)
    along_x[0] = xre
    along_x[1] = xim
    along_y[0] = yre
    along_y[1] = yim
    hre, him = coupled(tiles, kernel, table)
    field = inv_spectrum(hre, him, table)
    store_blocks(out, field)
    top = jnp.concatenate([hre[0:ROWS], him[0:ROWS]], axis=0).astype(bf16)
    top = jnp.concatenate([top, spectrum[0:ROWS], spectrum[64 : 64 + ROWS]], axis=0)
    a = mm(top, xre)
    b = mm(top, xim)
    a = a[0:64] + a[64:128]
    b = b[0:64] + b[64:128]
    pre = a[0:ROWS] - b[ROWS:64]
    pim = a[ROWS:64] + b[0:ROWS]
    sre = jnp.sum(pre * yre - pim * yim, axis=0, keepdims=True)
    sim = jnp.sum(pre * yim + pim * yre, axis=0, keepdims=True)
    total = jnp.concatenate([sre, sim], axis=1)
    high = total.astype(bf16).astype(f32)
    low = total - high
    row = lax.broadcasted_iota(jnp.int32, (8, 128), 0)
    extra = jnp.where(row == 0, high, jnp.where(row == 1, low, 0.0)).astype(bf16)
    for d in range(PEERS):
        out[d, ROWS : ROWS + 8, :] = extra


def back_body(tiles, kernel, table, measured, along_x, along_y, out):
    sums = jnp.zeros((8, 128), f32)
    for s in range(PEERS):
        sums = sums + tiles[s, ROWS : ROWS + 8, :].astype(f32)
    sums = sums[0:1] + sums[1:2]
    mre = sums[:, 0:RECV] - measured[0, 0:1, :]
    mim = sums[:, RECV : 2 * RECV] - measured[0, 1:2, :]
    yre = along_y[0]
    yim = along_y[1]
    mixed_re = mre * yre + mim * yim
    mixed_im = mim * yre - mre * yim
    mixed = jnp.concatenate([mixed_re, mixed_im], axis=0).astype(bf16)
    a = mm_nt(mixed, along_x[0])
    b = mm_nt(mixed, along_x[1])
    bre = (a[0:ROWS] + b[ROWS : 2 * ROWS]) * float(GRID)
    bim = (a[ROWS : 2 * ROWS] - b[0:ROWS]) * float(GRID)
    hre = []
    him = []
    for l in range(2):
        kre = kernel[0, 0, l].astype(f32)
        kim = kernel[1, 0, l].astype(f32)
        hre.append(kre * bre + kim * bim)
        him.append(kre * bim - kim * bre)
    field = inv_spectrum(jnp.concatenate(hre, axis=0), jnp.concatenate(him, axis=0), table)
    store_blocks(out, field)


def field_body(tiles, incident, table, out):
    dre, dim = inv_lines(lines_of(tiles), table)
    for part, delta in enumerate((dre, dim)):
        total = incident[64 * part : 64 * part + 64] + delta
        for l in range(2):
            out[0, part, :, l, :] = total[ROWS * l : ROWS * l + ROWS]


def gradient_body(tiles, field_tiles, incident, table, wave, out):
    dre, dim = inv_lines(lines_of(field_tiles), table)
    ure = incident[0:64] + dre
    uim = incident[64:128] + dim
    wave[0:64] = ure
    wave[64:128] = uim
    bre, bim = inv_lines(lines_of(tiles), table)
    gre = (ure * bre + uim * bim).astype(bf16)
    gim = (ure * bim - uim * bre).astype(bf16)
    for s in range(PEERS):
        row = ROWS * (s // 4)
        part = gre if row < 64 else gim
        out[SHARES.index(s)] = part[row % 64 : row % 64 + ROWS, 128 * (s % 4) : 128 * (s % 4) + 128]


def share_body(arrived, out):
    total = jnp.zeros((ROWS, 128), f32)
    for s in range(PEERS):
        total = total + arrived[s].astype(f32)
    total = total.astype(bf16)
    for d in range(2 * PEERS):
        out[d] = total


def update_body(shares, contrast, wave, table, updated, out):
    freqs = 2.0 * PEERS
    rows = []
    for group in range(4):
        lanes = []
        for s in range(4 * group, 4 * group + 4):
            z = s // 2
            core = s % 2
            pair = [shares[FREQS.index(4 * z + 2 * y + core)].astype(f32) for y in range(2)]
            lanes.append(pair[0] + pair[1])
        total = jnp.concatenate(lanes, axis=1)
        new = contrast[ROWS * group : ROWS * group + ROWS] - total / freqs
        updated[group // 2, :, group % 2, :] = new
        rows.append(new)
    cre = jnp.concatenate(rows[0:2], axis=0)
    cim = jnp.concatenate(rows[2:4], axis=0)
    vre, vim = times(cre, cim, wave[0:64], wave[64:128])
    wre, wim = fwd_lines(vre, vim, table)
    store_tiles(out, wre, wim)


TILES = ((PEERS, ROWS, 128), bf16)
LINES = ((128, GRID), f32)
IN_VMEM = pl.BlockSpec(memory_space=pltpu.VMEM)
IN_SMEM = pl.BlockSpec(memory_space=pltpu.SMEM)


IN_HBM = pl.BlockSpec(memory_space=pltpu.HBM)


def run(body, outs, *args, spaces=(), scratch=(), places=None):
    many = isinstance(outs, list)
    shapes = [jax.ShapeDtypeStruct(*o) for o in (outs if many else [outs])]
    spaces = list(spaces) + [IN_VMEM] * (len(args) - len(spaces))
    return pl.pallas_call(
        body,
        out_shape=shapes if many else shapes[0],
        in_specs=spaces,
        out_specs=places or ([IN_VMEM] * len(shapes) if many else IN_VMEM),
        scratch_shapes=scratch,
        compiler_params=pltpu.CompilerParams(vmem_limit_bytes=40 * 1024 * 1024),
    )(*args)


def stay(array):
    return pltpu.with_memory_space_constraint(array, pltpu.HBM)


def exchange(blocks, axis, groups):
    return lax.all_to_all(
        blocks, axis, split_axis=0, concat_axis=0, tiled=True, axis_index_groups=groups
    )


def local(contrast, green_kernel, source_pos, receiver_pos, measured):
    table = jnp.asarray(dft_tables())
    kernel = green_kernel[0]
    first = (lax.axis_index("plane") * ROWS).astype(jnp.int32)[None]

    source, spectrum, table, places, observed = run(
        source_body,
        [
            TILES,
            ((128, GRID), bf16),
            (table.shape, bf16),
            (receiver_pos.shape, jnp.int32),
            (measured.shape, f32),
        ],
        stay(source_pos),
        first,
        stay(kernel),
        stay(table),
        stay(receiver_pos),
        stay(measured),
        spaces=(IN_HBM, IN_SMEM, IN_HBM, IN_HBM, IN_HBM, IN_HBM),
        scratch=[
            pltpu.VMEM((2, 2, ROWS, GRID), bf16),
            pltpu.SMEM((1, 2), jnp.int32),
            pltpu.SemaphoreType.DMA((7,)),
        ],
    )
    arrived = exchange(source, "plane", [list(ORDER)])
    incident, lines, sent = run(first_line_body, [LINES, LINES, TILES], arrived, contrast, table)
    arrived = exchange(sent, "plane", [list(ORDER)])
    sent = run(spectral_body, TILES, arrived, kernel, table)
    arrived = exchange(sent, "plane", [list(ORDER)])
    sent = run(line_body, TILES, arrived, lines, incident, table)
    arrived = exchange(sent, "plane", [list(ORDER)])
    sent, along_x, along_y = run(
        sampled_body,
        [
            ((PEERS, ROWS + 8, 128), bf16),
            ((2, GRID, RECV), bf16),
            ((2, ROWS, RECV), f32),
        ],
        first,
        arrived,
        kernel,
        table,
        spectrum,
        places,
        spaces=(IN_SMEM,),
    )
    field = exchange(sent, "plane", [list(ORDER)])
    sent = run(back_body, TILES, field, kernel, table, observed, along_x, along_y)
    arrived = exchange(sent, "plane", [list(ORDER)])
    wave, sent = run(gradient_body, [LINES, TILES], arrived, field, incident, table)
    arrived = exchange(sent, "freq", [[4 * (s // 2) + 2 * y + s % 2 for s in SHARES] for y in range(2)])
    sent = run(share_body, ((2 * PEERS, ROWS, 128), bf16), arrived)
    arrived = exchange(sent, "freq", [list(FREQS)])
    updated, sent = run(
        update_body, [(contrast.shape, f32), TILES], arrived, lines, wave, table
    )
    arrived = exchange(sent, "plane", [list(ORDER)])
    sent, updated = run(
        last_spectral_body,
        [TILES, (contrast.shape, f32)],
        arrived,
        kernel,
        table,
        updated,
        scratch=[pltpu.SemaphoreType.DMA],
        places=[IN_VMEM, IN_HBM],
    )
    arrived = exchange(sent, "plane", [list(ORDER)])
    field = run(field_body, ((1,) + contrast.shape, f32), arrived, incident, table)
    return updated, field


def solution(mesh):
    return jax.shard_map(
        local,
        mesh=mesh,
        in_specs=(
            P(None, "plane", None, None),
            P("freq", None, None, None, "plane", None),
            P("freq", None),
            P("freq", None, None),
            P("freq", None, None),
        ),
        out_specs=(P(None, "plane", None, None), P("freq", None, "plane", None, None)),
        check_vma=False,
    )
```

```python
import math

import jax
import jax.numpy as jnp
import ml_dtypes
import numpy as np
from jax import lax
from jax.experimental import pallas as pl
from jax.experimental.pallas import tpu as pltpu
from jax.sharding import PartitionSpec as P

GRID = 512
ROWS = 32
PEERS = 16
RECV = 64
GAIN = 3.0
f32 = jnp.float32
bf16 = jnp.bfloat16

ORDER = (5, 12, 4, 3, 1, 13, 7, 0, 9, 2, 6, 11, 8, 15, 14, 10)
AT = tuple(ORDER.index(b) for b in range(PEERS))
SHARES = tuple(2 * z + c for c in (1, 0) for z in (7, 6, 5, 4, 3, 2, 1, 0))

FREQS = (
    19, 28, 4, 5, 13, 29, 1, 17, 7, 25, 9, 8, 12, 14, 0, 24,
    15, 2, 30, 23, 10, 20, 16, 22, 3, 27, 26, 11, 21, 18, 31, 6,
)


def dft_tables():
    k = np.arange(GRID, dtype=np.int64)
    angle = ((k[:, None] * k[None, :]) % GRID).astype(np.float32) * np.float32(2.0 * math.pi / GRID)
    scale = np.float32(1.0 / math.sqrt(GRID))
    both = np.stack([np.cos(angle) * scale, np.sin(angle) * scale])
    return both.astype(ml_dtypes.bfloat16)


def mm(a, b):
    return jnp.dot(a, b, preferred_element_type=f32)


def mm_nt(a, b):
    return lax.dot_general(a, b, (((1,), (1,)), ((), ())), preferred_element_type=f32)


def swap_groups(x):
    lane = lax.broadcasted_iota(jnp.int32, x[0].shape, 1)
    low = lane < 64
    even = (lane & 32) == 0
    a0 = jnp.where(low, x[0], pltpu.roll(x[2], 64, 1))
    a2 = jnp.where(low, pltpu.roll(x[0], 64, 1), x[2])
    a1 = jnp.where(low, x[1], pltpu.roll(x[3], 64, 1))
    a3 = jnp.where(low, pltpu.roll(x[1], 64, 1), x[3])
    y0 = jnp.where(even, a0, pltpu.roll(a1, 32, 1))
    y1 = jnp.where(even, pltpu.roll(a0, 96, 1), a1)
    y2 = jnp.where(even, a2, pltpu.roll(a3, 32, 1))
    y3 = jnp.where(even, pltpu.roll(a2, 96, 1), a3)
    return [y0, y1, y2, y3]


def lines_of(tiles):
    parts = [[], [], [], []]
    for g in range(4):
        swapped = swap_groups([tiles[AT[4 * g + i], 0:ROWS, :].astype(f32) for i in range(4)])
        for j in range(4):
            parts[j].append(swapped[j])
    return jnp.concatenate([jnp.concatenate(p, axis=1) for p in parts], axis=0).astype(bf16)


def store_tiles(out, re, im):
    quarter = [re[0:ROWS], re[ROWS:], im[0:ROWS], im[ROWS:]]
    for g in range(4):
        swapped = swap_groups([q[:, 128 * g : 128 * g + 128] for q in quarter])
        for j in range(4):
            out[AT[4 * g + j]] = swapped[j].astype(bf16)


def inv_lines(lines, table):
    a = mm(lines, table[0])
    b = mm(lines, table[1])
    return a[0:64] - b[64:128], a[64:128] + b[0:64]


def fwd_lines(re, im, table):
    both = jnp.concatenate([re, im], axis=0).astype(bf16)
    a = mm(both, table[0])
    b = mm(both, table[1])
    return a[0:64] + b[64:128], a[64:128] - b[0:64]


def times(cre, cim, ure, uim):
    return cre * ure - cim * uim, cre * uim + cim * ure


def inv_spectrum(hre, him, table):
    straight = jnp.concatenate([hre, him], axis=0).astype(bf16)
    crossed = jnp.concatenate([-him, hre], axis=0).astype(bf16)
    return mm_nt(table[0], straight) + mm_nt(table[1], crossed)


def store_blocks(out, field):
    field = field.astype(bf16)
    for d in range(PEERS):
        out[AT[d], 0:ROWS, :] = field[ROWS * d : ROWS * d + ROWS]


def couple(kernel, fre, fim):
    hre = []
    him = []
    for lo in range(2):
        sre = None
        sim = None
        for li in range(2):
            kre = kernel[0, lo, li].astype(f32)
            kim = kernel[1, lo, li].astype(f32)
            vre = fre[ROWS * li : ROWS * li + ROWS]
            vim = fim[ROWS * li : ROWS * li + ROWS]
            pre, pim = times(kre, kim, vre, vim)
            sre = pre if sre is None else sre + pre
            sim = pim if sim is None else sim + pim
        hre.append(sre)
        him.append(sim)
    return jnp.concatenate(hre, axis=0), jnp.concatenate(him, axis=0)


def source_body(
    spot_hbm,
    first,
    kernel_hbm,
    table_hbm,
    places_hbm,
    measured_hbm,
    out,
    spectrum,
    table,
    places,
    measured,
    kernel,
    spot,
    sems,
):
    copies = []
    where = pltpu.make_async_copy(spot_hbm, spot, sems.at[4])
    where.start()
    for part in range(2):
        copies.append(
            pltpu.make_async_copy(
                kernel_hbm.at[part, :, 0], kernel.at[part], sems.at[part]
            )
        )
        copies.append(
            pltpu.make_async_copy(table_hbm.at[part], table.at[part], sems.at[2 + part])
        )
    for copy in (copies[0], copies[2], copies[1], copies[3]):
        copy.start()
    extra = [
        pltpu.make_async_copy(places_hbm, places, sems.at[5]),
        pltpu.make_async_copy(measured_hbm, measured, sems.at[6]),
    ]
    for copy in extra:
        copy.start()
    where.wait()
    x0 = spot[0, 0]
    y0 = spot[0, 1]
    step = 2.0 * math.pi / GRID
    kx = lax.broadcasted_iota(jnp.int32, (8, GRID), 1)
    ax = ((kx * x0) & (GRID - 1)).astype(f32) * step
    ky = lax.broadcasted_iota(jnp.int32, (ROWS, 128), 0) + first[0]
    ay = ((ky * y0) & (GRID - 1)).astype(f32) * step
    xre = jnp.cos(ax)[0:1]
    xim = -jnp.sin(ax)[0:1]
    yre = jnp.cos(ay)[:, 0:1]
    yim = -jnp.sin(ay)[:, 0:1]
    qre = GAIN * (yre * xre - yim * xim)
    qim = GAIN * (yre * xim + yim * xre)
    copies[0].wait()
    copies[2].wait()
    zre = []
    zim = []
    for lo in range(2):
        a, b = times(kernel[0, lo].astype(f32), kernel[1, lo].astype(f32), qre, qim)
        zre.append(a)
        zim.append(b)
    zre = jnp.concatenate(zre, axis=0)
    zim = jnp.concatenate(zim, axis=0)
    straight = jnp.concatenate([zre, zim], axis=0).astype(bf16)
    crossed = jnp.concatenate([-zim, zre], axis=0).astype(bf16)
    spectrum[...] = straight
    copies[1].wait()
    field = mm_nt(table[0], straight)
    copies[3].wait()
    field = field + mm_nt(table[1], crossed)
    store_blocks(out, field)
    for copy in extra:
        copy.wait()


def by_part_layer(field, part):
    return jnp.concatenate([field[part, :, 0, :], field[part, :, 1, :]], axis=0)


def first_line_body(tiles, contrast, table, incident, lines, out):
    ure, uim = inv_lines(lines_of(tiles), table)
    incident[0:64] = ure
    incident[64:128] = uim
    cre = by_part_layer(contrast, 0)
    cim = by_part_layer(contrast, 1)
    lines[0:64] = cre
    lines[64:128] = cim
    vre, vim = times(cre, cim, ure, uim)
    wre, wim = fwd_lines(vre, vim, table)
    store_tiles(out, wre, wim)


def line_body(tiles, contrast, incident, table, out):
    dre, dim = inv_lines(lines_of(tiles), table)
    ure = incident[0:64] + dre
    uim = incident[64:128] + dim
    vre, vim = times(contrast[0:64], contrast[64:128], ure, uim)
    wre, wim = fwd_lines(vre, vim, table)
    store_tiles(out, wre, wim)


def coupled(tiles, kernel, table):
    stacked = jnp.concatenate([tiles[AT[d]] for d in range(PEERS)], axis=0)
    turned = stacked.T
    a = mm(turned, table[0])
    b = mm(turned, table[1])
    fre = a[0:64] + b[64:128]
    fim = a[64:128] - b[0:64]
    return couple(kernel, fre, fim)


def spectral_body(tiles, kernel, table, out):
    hre, him = coupled(tiles, kernel, table)
    field = inv_spectrum(hre, him, table)
    store_blocks(out, field)


def last_spectral_body(tiles, kernel, table, updated, out, updated_hbm, sem):
    copy = pltpu.make_async_copy(updated, updated_hbm, sem)
    copy.start()
    spectral_body(tiles, kernel, table, out)
    copy.wait()


def sampled_body(first, tiles, kernel, table, spectrum, places, out, along_x, along_y):
    where = lax.broadcasted_iota(jnp.int32, (GRID, RECV), 0)
    at_x = jnp.where(where == places[0, 0:1, :], 1.0, 0.0).astype(bf16)
    at_y = jnp.where(where == places[0, 1:2, :], 1.0, 0.0).astype(bf16)
    start = pl.multiple_of(first[0], ROWS)
    xre = mm(table[0], at_x).astype(bf16)
    xim = mm(table[1], at_x).astype(bf16)
    yre = mm(table[0, pl.ds(start, ROWS), :], at_y)
    yim = mm(table[1, pl.ds(start, ROWS), :], at_y)
    along_x[0] = xre
    along_x[1] = xim
    along_y[0] = yre
    along_y[1] = yim
    hre, him = coupled(tiles, kernel, table)
    field = inv_spectrum(hre, him, table)
    store_blocks(out, field)
    top = jnp.concatenate([hre[0:ROWS], him[0:ROWS]], axis=0).astype(bf16)
    top = jnp.concatenate([top, spectrum[0:ROWS], spectrum[64 : 64 + ROWS]], axis=0)
    a = mm(top, xre)
    b = mm(top, xim)
    a = a[0:64] + a[64:128]
    b = b[0:64] + b[64:128]
    pre = a[0:ROWS] - b[ROWS:64]
    pim = a[ROWS:64] + b[0:ROWS]
    sre = jnp.sum(pre * yre - pim * yim, axis=0, keepdims=True)
    sim = jnp.sum(pre * yim + pim * yre, axis=0, keepdims=True)
    total = jnp.concatenate([sre, sim], axis=1)
    high = total.astype(bf16).astype(f32)
    low = total - high
    row = lax.broadcasted_iota(jnp.int32, (8, 128), 0)
    extra = jnp.where(row == 0, high, jnp.where(row == 1, low, 0.0)).astype(bf16)
    for d in range(PEERS):
        out[d, ROWS : ROWS + 8, :] = extra


def back_body(tiles, kernel, table, measured, along_x, along_y, out):
    sums = jnp.zeros((8, 128), f32)
    for s in range(PEERS):
        sums = sums + tiles[s, ROWS : ROWS + 8, :].astype(f32)
    sums = sums[0:1] + sums[1:2]
    mre = sums[:, 0:RECV] - measured[0, 0:1, :]
    mim = sums[:, RECV : 2 * RECV] - measured[0, 1:2, :]
    yre = along_y[0]
    yim = along_y[1]
    mixed_re = mre * yre + mim * yim
    mixed_im = mim * yre - mre * yim
    mixed = jnp.concatenate([mixed_re, mixed_im], axis=0).astype(bf16)
    a = mm_nt(mixed, along_x[0])
    b = mm_nt(mixed, along_x[1])
    bre = (a[0:ROWS] + b[ROWS : 2 * ROWS]) * float(GRID)
    bim = (a[ROWS : 2 * ROWS] - b[0:ROWS]) * float(GRID)
    hre = []
    him = []
    for l in range(2):
        kre = kernel[0, 0, l].astype(f32)
        kim = kernel[1, 0, l].astype(f32)
        hre.append(kre * bre + kim * bim)
        him.append(kre * bim - kim * bre)
    field = inv_spectrum(jnp.concatenate(hre, axis=0), jnp.concatenate(him, axis=0), table)
    store_blocks(out, field)


def field_body(tiles, incident, table, out):
    dre, dim = inv_lines(lines_of(tiles), table)
    for part, delta in enumerate((dre, dim)):
        total = incident[64 * part : 64 * part + 64] + delta
        for l in range(2):
            out[0, part, :, l, :] = total[ROWS * l : ROWS * l + ROWS]


def gradient_body(tiles, field_tiles, incident, table, wave, out):
    dre, dim = inv_lines(lines_of(field_tiles), table)
    ure = incident[0:64] + dre
    uim = incident[64:128] + dim
    wave[0:64] = ure
    wave[64:128] = uim
    bre, bim = inv_lines(lines_of(tiles), table)
    gre = (ure * bre + uim * bim).astype(bf16)
    gim = (ure * bim - uim * bre).astype(bf16)
    for s in range(PEERS):
        row = ROWS * (s // 4)
        part = gre if row < 64 else gim
        out[SHARES.index(s)] = part[row % 64 : row % 64 + ROWS, 128 * (s % 4) : 128 * (s % 4) + 128]


def share_body(arrived, out):
    total = jnp.zeros((ROWS, 128), f32)
    for s in range(PEERS):
        total = total + arrived[s].astype(f32)
    total = total.astype(bf16)
    for d in range(2 * PEERS):
        out[d] = total


def update_body(shares, contrast, wave, table, updated, out):
    freqs = 2.0 * PEERS
    rows = []
    for group in range(4):
        lanes = []
        for s in range(4 * group, 4 * group + 4):
            z = s // 2
            core = s % 2
            pair = [shares[FREQS.index(4 * z + 2 * y + core)].astype(f32) for y in range(2)]
            lanes.append(pair[0] + pair[1])
        total = jnp.concatenate(lanes, axis=1)
        new = contrast[ROWS * group : ROWS * group + ROWS] - total / freqs
        updated[group // 2, :, group % 2, :] = new
        rows.append(new)
    cre = jnp.concatenate(rows[0:2], axis=0)
    cim = jnp.concatenate(rows[2:4], axis=0)
    vre, vim = times(cre, cim, wave[0:64], wave[64:128])
    wre, wim = fwd_lines(vre, vim, table)
    store_tiles(out, wre, wim)


TILES = ((PEERS, ROWS, 128), bf16)
LINES = ((128, GRID), f32)
IN_VMEM = pl.BlockSpec(memory_space=pltpu.VMEM)
IN_SMEM = pl.BlockSpec(memory_space=pltpu.SMEM)


IN_HBM = pl.BlockSpec(memory_space=pltpu.HBM)


def run(body, outs, *args, spaces=(), scratch=(), places=None):
    many = isinstance(outs, list)
    shapes = [jax.ShapeDtypeStruct(*o) for o in (outs if many else [outs])]
    spaces = list(spaces) + [IN_VMEM] * (len(args) - len(spaces))
    return pl.pallas_call(
        body,
        out_shape=shapes if many else shapes[0],
        in_specs=spaces,
        out_specs=places or ([IN_VMEM] * len(shapes) if many else IN_VMEM),
        scratch_shapes=scratch,
        compiler_params=pltpu.CompilerParams(vmem_limit_bytes=40 * 1024 * 1024),
    )(*args)


def stay(array):
    return pltpu.with_memory_space_constraint(array, pltpu.HBM)


def exchange(blocks, axis, groups):
    return lax.all_to_all(
        blocks, axis, split_axis=0, concat_axis=0, tiled=True, axis_index_groups=groups
    )


def local(contrast, green_kernel, source_pos, receiver_pos, measured):
    table = jnp.asarray(dft_tables())
    kernel = green_kernel[0]
    first = (lax.axis_index("plane") * ROWS).astype(jnp.int32)[None]

    source, spectrum, table, places, observed = run(
        source_body,
        [
            TILES,
            ((128, GRID), bf16),
            (table.shape, bf16),
            (receiver_pos.shape, jnp.int32),
            (measured.shape, f32),
        ],
        stay(source_pos),
        first,
        stay(kernel),
        stay(table),
        stay(receiver_pos),
        stay(measured),
        spaces=(IN_HBM, IN_SMEM, IN_HBM, IN_HBM, IN_HBM, IN_HBM),
        scratch=[
            pltpu.VMEM((2, 2, ROWS, GRID), bf16),
            pltpu.SMEM((1, 2), jnp.int32),
            pltpu.SemaphoreType.DMA((7,)),
        ],
    )
    arrived = exchange(source, "plane", [list(ORDER)])
    incident, lines, sent = run(first_line_body, [LINES, LINES, TILES], arrived, contrast, table)
    arrived = exchange(sent, "plane", [list(ORDER)])
    sent = run(spectral_body, TILES, arrived, kernel, table)
    arrived = exchange(sent, "plane", [list(ORDER)])
    sent = run(line_body, TILES, arrived, lines, incident, table)
    arrived = exchange(sent, "plane", [list(ORDER)])
    sent, along_x, along_y = run(
        sampled_body,
        [
            ((PEERS, ROWS + 8, 128), bf16),
            ((2, GRID, RECV), bf16),
            ((2, ROWS, RECV), f32),
        ],
        first,
        arrived,
        kernel,
        table,
        spectrum,
        places,
        spaces=(IN_SMEM,),
    )
    field = exchange(sent, "plane", [list(ORDER)])
    sent = run(back_body, TILES, field, kernel, table, observed, along_x, along_y)
    arrived = exchange(sent, "plane", [list(ORDER)])
    wave, sent = run(gradient_body, [LINES, TILES], arrived, field, incident, table)
    arrived = exchange(sent, "freq", [[4 * (s // 2) + 2 * y + s % 2 for s in SHARES] for y in range(2)])
    sent = run(share_body, ((2 * PEERS, ROWS, 128), bf16), arrived)
    arrived = exchange(sent, "freq", [list(FREQS)])
    updated, sent = run(
        update_body, [(contrast.shape, f32), TILES], arrived, lines, wave, table
    )
    arrived = exchange(sent, "plane", [list(ORDER)])
    sent, updated = run(
        last_spectral_body,
        [TILES, (contrast.shape, f32)],
        arrived,
        kernel,
        table,
        updated,
        scratch=[pltpu.SemaphoreType.DMA],
        places=[IN_VMEM, IN_HBM],
    )
    arrived = exchange(sent, "plane", [list(ORDER)])
    field = run(field_body, ((1,) + contrast.shape, f32), arrived, incident, table)
    return updated, field


def solution(mesh):
    return jax.shard_map(
        local,
        mesh=mesh,
        in_specs=(
            P(None, "plane", None, None),
            P("freq", None, None, None, "plane", None),
            P("freq", None),
            P("freq", None, None),
            P("freq", None, None),
        ),
        out_specs=(P(None, "plane", None, None), P("freq", None, "plane", None, None)),
        check_vma=False,
    )
```

```python
import math

import jax
import jax.numpy as jnp
import ml_dtypes
import numpy as np
from jax import lax
from jax.experimental import pallas as pl
from jax.experimental.pallas import tpu as pltpu
from jax.sharding import PartitionSpec as P

GRID = 512
ROWS = 32
PEERS = 16
RECV = 64
GAIN = 3.0
f32 = jnp.float32
bf16 = jnp.bfloat16

ORDER = (5, 12, 4, 3, 1, 13, 7, 0, 9, 2, 6, 11, 8, 15, 14, 10)
AT = tuple(ORDER.index(b) for b in range(PEERS))
SHARES = tuple(2 * z + c for c in (0, 1) for z in (7, 6, 5, 4, 3, 2, 1, 0))

FREQS = (
    19, 28, 4, 5, 13, 29, 1, 17, 7, 25, 9, 8, 12, 14, 0, 24,
    15, 2, 30, 23, 10, 20, 16, 22, 3, 27, 26, 11, 21, 18, 31, 6,
)


def dft_tables():
    k = np.arange(GRID, dtype=np.int64)
    angle = ((k[:, None] * k[None, :]) % GRID).astype(np.float32) * np.float32(2.0 * math.pi / GRID)
    scale = np.float32(1.0 / math.sqrt(GRID))
    both = np.stack([np.cos(angle) * scale, np.sin(angle) * scale])
    return both.astype(ml_dtypes.bfloat16)


def mm(a, b):
    return jnp.dot(a, b, preferred_element_type=f32)


def mm_nt(a, b):
    return lax.dot_general(a, b, (((1,), (1,)), ((), ())), preferred_element_type=f32)


def swap_groups(x):
    lane = lax.broadcasted_iota(jnp.int32, x[0].shape, 1)
    low = lane < 64
    even = (lane & 32) == 0
    a0 = jnp.where(low, x[0], pltpu.roll(x[2], 64, 1))
    a2 = jnp.where(low, pltpu.roll(x[0], 64, 1), x[2])
    a1 = jnp.where(low, x[1], pltpu.roll(x[3], 64, 1))
    a3 = jnp.where(low, pltpu.roll(x[1], 64, 1), x[3])
    y0 = jnp.where(even, a0, pltpu.roll(a1, 32, 1))
    y1 = jnp.where(even, pltpu.roll(a0, 96, 1), a1)
    y2 = jnp.where(even, a2, pltpu.roll(a3, 32, 1))
    y3 = jnp.where(even, pltpu.roll(a2, 96, 1), a3)
    return [y0, y1, y2, y3]


def lines_of(tiles):
    parts = [[], [], [], []]
    for g in range(4):
        swapped = swap_groups([tiles[AT[4 * g + i], 0:ROWS, :].astype(f32) for i in range(4)])
        for j in range(4):
            parts[j].append(swapped[j])
    return jnp.concatenate([jnp.concatenate(p, axis=1) for p in parts], axis=0).astype(bf16)


def store_tiles(out, re, im):
    quarter = [re[0:ROWS], re[ROWS:], im[0:ROWS], im[ROWS:]]
    for g in range(4):
        swapped = swap_groups([q[:, 128 * g : 128 * g + 128] for q in quarter])
        for j in range(4):
            out[AT[4 * g + j]] = swapped[j].astype(bf16)


def inv_lines(lines, table):
    a = mm(lines, table[0])
    b = mm(lines, table[1])
    return a[0:64] - b[64:128], a[64:128] + b[0:64]


def fwd_lines(re, im, table):
    both = jnp.concatenate([re, im], axis=0).astype(bf16)
    a = mm(both, table[0])
    b = mm(both, table[1])
    return a[0:64] + b[64:128], a[64:128] - b[0:64]


def times(cre, cim, ure, uim):
    return cre * ure - cim * uim, cre * uim + cim * ure


def inv_spectrum(hre, him, table):
    straight = jnp.concatenate([hre, him], axis=0).astype(bf16)
    crossed = jnp.concatenate([-him, hre], axis=0).astype(bf16)
    return mm_nt(table[0], straight) + mm_nt(table[1], crossed)


def store_blocks(out, field):
    field = field.astype(bf16)
    for d in range(PEERS):
        out[AT[d], 0:ROWS, :] = field[ROWS * d : ROWS * d + ROWS]


def couple(kernel, fre, fim):
    hre = []
    him = []
    for lo in range(2):
        sre = None
        sim = None
        for li in range(2):
            kre = kernel[0, lo, li].astype(f32)
            kim = kernel[1, lo, li].astype(f32)
            vre = fre[ROWS * li : ROWS * li + ROWS]
            vim = fim[ROWS * li : ROWS * li + ROWS]
            pre, pim = times(kre, kim, vre, vim)
            sre = pre if sre is None else sre + pre
            sim = pim if sim is None else sim + pim
        hre.append(sre)
        him.append(sim)
    return jnp.concatenate(hre, axis=0), jnp.concatenate(him, axis=0)


def source_body(
    spot_hbm,
    first,
    kernel_hbm,
    table_hbm,
    places_hbm,
    measured_hbm,
    out,
    spectrum,
    table,
    places,
    measured,
    kernel,
    spot,
    sems,
):
    copies = []
    where = pltpu.make_async_copy(spot_hbm, spot, sems.at[4])
    where.start()
    for part in range(2):
        copies.append(
            pltpu.make_async_copy(
                kernel_hbm.at[part, :, 0], kernel.at[part], sems.at[part]
            )
        )
        copies.append(
            pltpu.make_async_copy(table_hbm.at[part], table.at[part], sems.at[2 + part])
        )
    for copy in (copies[0], copies[2], copies[1], copies[3]):
        copy.start()
    extra = [
        pltpu.make_async_copy(places_hbm, places, sems.at[5]),
        pltpu.make_async_copy(measured_hbm, measured, sems.at[6]),
    ]
    for copy in extra:
        copy.start()
    where.wait()
    x0 = spot[0, 0]
    y0 = spot[0, 1]
    step = 2.0 * math.pi / GRID
    kx = lax.broadcasted_iota(jnp.int32, (8, GRID), 1)
    ax = ((kx * x0) & (GRID - 1)).astype(f32) * step
    ky = lax.broadcasted_iota(jnp.int32, (ROWS, 128), 0) + first[0]
    ay = ((ky * y0) & (GRID - 1)).astype(f32) * step
    xre = jnp.cos(ax)[0:1]
    xim = -jnp.sin(ax)[0:1]
    yre = jnp.cos(ay)[:, 0:1]
    yim = -jnp.sin(ay)[:, 0:1]
    qre = GAIN * (yre * xre - yim * xim)
    qim = GAIN * (yre * xim + yim * xre)
    copies[0].wait()
    copies[2].wait()
    zre = []
    zim = []
    for lo in range(2):
        a, b = times(kernel[0, lo].astype(f32), kernel[1, lo].astype(f32), qre, qim)
        zre.append(a)
        zim.append(b)
    zre = jnp.concatenate(zre, axis=0)
    zim = jnp.concatenate(zim, axis=0)
    straight = jnp.concatenate([zre, zim], axis=0).astype(bf16)
    crossed = jnp.concatenate([-zim, zre], axis=0).astype(bf16)
    spectrum[...] = straight
    copies[1].wait()
    field = mm_nt(table[0], straight)
    copies[3].wait()
    field = field + mm_nt(table[1], crossed)
    store_blocks(out, field)
    for copy in extra:
        copy.wait()


def by_part_layer(field, part):
    return jnp.concatenate([field[part, :, 0, :], field[part, :, 1, :]], axis=0)


def first_line_body(tiles, contrast, table, incident, lines, out):
    ure, uim = inv_lines(lines_of(tiles), table)
    incident[0:64] = ure
    incident[64:128] = uim
    cre = by_part_layer(contrast, 0)
    cim = by_part_layer(contrast, 1)
    lines[0:64] = cre
    lines[64:128] = cim
    vre, vim = times(cre, cim, ure, uim)
    wre, wim = fwd_lines(vre, vim, table)
    store_tiles(out, wre, wim)


def line_body(tiles, contrast, incident, table, out):
    dre, dim = inv_lines(lines_of(tiles), table)
    ure = incident[0:64] + dre
    uim = incident[64:128] + dim
    vre, vim = times(contrast[0:64], contrast[64:128], ure, uim)
    wre, wim = fwd_lines(vre, vim, table)
    store_tiles(out, wre, wim)


def coupled(tiles, kernel, table):
    stacked = jnp.concatenate([tiles[AT[d]] for d in range(PEERS)], axis=0)
    turned = stacked.T
    a = mm(turned, table[0])
    b = mm(turned, table[1])
    fre = a[0:64] + b[64:128]
    fim = a[64:128] - b[0:64]
    return couple(kernel, fre, fim)


def spectral_body(tiles, kernel, table, out):
    hre, him = coupled(tiles, kernel, table)
    field = inv_spectrum(hre, him, table)
    store_blocks(out, field)


def last_spectral_body(tiles, kernel, table, updated, out, updated_hbm, sem):
    copy = pltpu.make_async_copy(updated, updated_hbm, sem)
    copy.start()
    spectral_body(tiles, kernel, table, out)
    copy.wait()


def sampled_body(first, tiles, kernel, table, spectrum, places, out, along_x, along_y):
    where = lax.broadcasted_iota(jnp.int32, (GRID, RECV), 0)
    at_x = jnp.where(where == places[0, 0:1, :], 1.0, 0.0).astype(bf16)
    at_y = jnp.where(where == places[0, 1:2, :], 1.0, 0.0).astype(bf16)
    start = pl.multiple_of(first[0], ROWS)
    xre = mm(table[0], at_x).astype(bf16)
    xim = mm(table[1], at_x).astype(bf16)
    yre = mm(table[0, pl.ds(start, ROWS), :], at_y)
    yim = mm(table[1, pl.ds(start, ROWS), :], at_y)
    along_x[0] = xre
    along_x[1] = xim
    along_y[0] = yre
    along_y[1] = yim
    hre, him = coupled(tiles, kernel, table)
    field = inv_spectrum(hre, him, table)
    store_blocks(out, field)
    top = jnp.concatenate([hre[0:ROWS], him[0:ROWS]], axis=0).astype(bf16)
    top = jnp.concatenate([top, spectrum[0:ROWS], spectrum[64 : 64 + ROWS]], axis=0)
    a = mm(top, xre)
    b = mm(top, xim)
    a = a[0:64] + a[64:128]
    b = b[0:64] + b[64:128]
    pre = a[0:ROWS] - b[ROWS:64]
    pim = a[ROWS:64] + b[0:ROWS]
    sre = jnp.sum(pre * yre - pim * yim, axis=0, keepdims=True)
    sim = jnp.sum(pre * yim + pim * yre, axis=0, keepdims=True)
    total = jnp.concatenate([sre, sim], axis=1)
    high = total.astype(bf16).astype(f32)
    low = total - high
    row = lax.broadcasted_iota(jnp.int32, (8, 128), 0)
    extra = jnp.where(row == 0, high, jnp.where(row == 1, low, 0.0)).astype(bf16)
    for d in range(PEERS):
        out[d, ROWS : ROWS + 8, :] = extra


def back_body(tiles, kernel, table, measured, along_x, along_y, out):
    sums = jnp.zeros((8, 128), f32)
    for s in range(PEERS):
        sums = sums + tiles[s, ROWS : ROWS + 8, :].astype(f32)
    sums = sums[0:1] + sums[1:2]
    mre = sums[:, 0:RECV] - measured[0, 0:1, :]
    mim = sums[:, RECV : 2 * RECV] - measured[0, 1:2, :]
    yre = along_y[0]
    yim = along_y[1]
    mixed_re = mre * yre + mim * yim
    mixed_im = mim * yre - mre * yim
    mixed = jnp.concatenate([mixed_re, mixed_im], axis=0).astype(bf16)
    a = mm_nt(mixed, along_x[0])
    b = mm_nt(mixed, along_x[1])
    bre = (a[0:ROWS] + b[ROWS : 2 * ROWS]) * float(GRID)
    bim = (a[ROWS : 2 * ROWS] - b[0:ROWS]) * float(GRID)
    hre = []
    him = []
    for l in range(2):
        kre = kernel[0, 0, l].astype(f32)
        kim = kernel[1, 0, l].astype(f32)
        hre.append(kre * bre + kim * bim)
        him.append(kre * bim - kim * bre)
    field = inv_spectrum(jnp.concatenate(hre, axis=0), jnp.concatenate(him, axis=0), table)
    store_blocks(out, field)


def field_body(tiles, incident, table, out):
    dre, dim = inv_lines(lines_of(tiles), table)
    for part, delta in enumerate((dre, dim)):
        total = incident[64 * part : 64 * part + 64] + delta
        for l in range(2):
            out[0, part, :, l, :] = total[ROWS * l : ROWS * l + ROWS]


def gradient_body(tiles, field_tiles, incident, table, wave, out):
    dre, dim = inv_lines(lines_of(field_tiles), table)
    ure = incident[0:64] + dre
    uim = incident[64:128] + dim
    wave[0:64] = ure
    wave[64:128] = uim
    bre, bim = inv_lines(lines_of(tiles), table)
    gre = (ure * bre + uim * bim).astype(bf16)
    gim = (ure * bim - uim * bre).astype(bf16)
    for s in range(PEERS):
        row = ROWS * (s // 4)
        part = gre if row < 64 else gim
        out[SHARES.index(s)] = part[row % 64 : row % 64 + ROWS, 128 * (s % 4) : 128 * (s % 4) + 128]


def share_body(arrived, out):
    total = jnp.zeros((ROWS, 128), f32)
    for s in range(PEERS):
        total = total + arrived[s].astype(f32)
    total = total.astype(bf16)
    for d in range(2 * PEERS):
        out[d] = total


def update_body(shares, contrast, wave, table, updated, out):
    freqs = 2.0 * PEERS
    rows = []
    for group in range(4):
        lanes = []
        for s in range(4 * group, 4 * group + 4):
            z = s // 2
            core = s % 2
            pair = [shares[FREQS.index(4 * z + 2 * y + core)].astype(f32) for y in range(2)]
            lanes.append(pair[0] + pair[1])
        total = jnp.concatenate(lanes, axis=1)
        new = contrast[ROWS * group : ROWS * group + ROWS] - total / freqs
        updated[group // 2, :, group % 2, :] = new
        rows.append(new)
    cre = jnp.concatenate(rows[0:2], axis=0)
    cim = jnp.concatenate(rows[2:4], axis=0)
    vre, vim = times(cre, cim, wave[0:64], wave[64:128])
    wre, wim = fwd_lines(vre, vim, table)
    store_tiles(out, wre, wim)


TILES = ((PEERS, ROWS, 128), bf16)
LINES = ((128, GRID), f32)
IN_VMEM = pl.BlockSpec(memory_space=pltpu.VMEM)
IN_SMEM = pl.BlockSpec(memory_space=pltpu.SMEM)


IN_HBM = pl.BlockSpec(memory_space=pltpu.HBM)


def run(body, outs, *args, spaces=(), scratch=(), places=None):
    many = isinstance(outs, list)
    shapes = [jax.ShapeDtypeStruct(*o) for o in (outs if many else [outs])]
    spaces = list(spaces) + [IN_VMEM] * (len(args) - len(spaces))
    return pl.pallas_call(
        body,
        out_shape=shapes if many else shapes[0],
        in_specs=spaces,
        out_specs=places or ([IN_VMEM] * len(shapes) if many else IN_VMEM),
        scratch_shapes=scratch,
        compiler_params=pltpu.CompilerParams(vmem_limit_bytes=40 * 1024 * 1024),
    )(*args)


def stay(array):
    return pltpu.with_memory_space_constraint(array, pltpu.HBM)


def exchange(blocks, axis, groups):
    return lax.all_to_all(
        blocks, axis, split_axis=0, concat_axis=0, tiled=True, axis_index_groups=groups
    )


def local(contrast, green_kernel, source_pos, receiver_pos, measured):
    table = jnp.asarray(dft_tables())
    kernel = green_kernel[0]
    first = (lax.axis_index("plane") * ROWS).astype(jnp.int32)[None]

    source, spectrum, table, places, observed = run(
        source_body,
        [
            TILES,
            ((128, GRID), bf16),
            (table.shape, bf16),
            (receiver_pos.shape, jnp.int32),
            (measured.shape, f32),
        ],
        stay(source_pos),
        first,
        stay(kernel),
        stay(table),
        stay(receiver_pos),
        stay(measured),
        spaces=(IN_HBM, IN_SMEM, IN_HBM, IN_HBM, IN_HBM, IN_HBM),
        scratch=[
            pltpu.VMEM((2, 2, ROWS, GRID), bf16),
            pltpu.SMEM((1, 2), jnp.int32),
            pltpu.SemaphoreType.DMA((7,)),
        ],
    )
    arrived = exchange(source, "plane", [list(ORDER)])
    incident, lines, sent = run(first_line_body, [LINES, LINES, TILES], arrived, contrast, table)
    arrived = exchange(sent, "plane", [list(ORDER)])
    sent = run(spectral_body, TILES, arrived, kernel, table)
    arrived = exchange(sent, "plane", [list(ORDER)])
    sent = run(line_body, TILES, arrived, lines, incident, table)
    arrived = exchange(sent, "plane", [list(ORDER)])
    sent, along_x, along_y = run(
        sampled_body,
        [
            ((PEERS, ROWS + 8, 128), bf16),
            ((2, GRID, RECV), bf16),
            ((2, ROWS, RECV), f32),
        ],
        first,
        arrived,
        kernel,
        table,
        spectrum,
        places,
        spaces=(IN_SMEM,),
    )
    field = exchange(sent, "plane", [list(ORDER)])
    sent = run(back_body, TILES, field, kernel, table, observed, along_x, along_y)
    arrived = exchange(sent, "plane", [list(ORDER)])
    wave, sent = run(gradient_body, [LINES, TILES], arrived, field, incident, table)
    arrived = exchange(sent, "freq", [[4 * (s // 2) + 2 * y + s % 2 for s in SHARES] for y in range(2)])
    sent = run(share_body, ((2 * PEERS, ROWS, 128), bf16), arrived)
    arrived = exchange(sent, "freq", [list(FREQS)])
    updated, sent = run(
        update_body, [(contrast.shape, f32), TILES], arrived, lines, wave, table
    )
    arrived = exchange(sent, "plane", [list(ORDER)])
    sent, updated = run(
        last_spectral_body,
        [TILES, (contrast.shape, f32)],
        arrived,
        kernel,
        table,
        updated,
        scratch=[pltpu.SemaphoreType.DMA],
        places=[IN_VMEM, IN_HBM],
    )
    arrived = exchange(sent, "plane", [list(ORDER)])
    field = run(field_body, ((1,) + contrast.shape, f32), arrived, incident, table)
    return updated, field


def solution(mesh):
    return jax.shard_map(
        local,
        mesh=mesh,
        in_specs=(
            P(None, "plane", None, None),
            P("freq", None, None, None, "plane", None),
            P("freq", None),
            P("freq", None, None),
            P("freq", None, None),
        ),
        out_specs=(P(None, "plane", None, None), P("freq", None, "plane", None, None)),
        check_vma=False,
    )
```
